32 devices in a mesh: dp: 8 (over z, x), table: 4 (over y, core).
Axes of the slice: x: 2, y: 2, z: 4, core: 2. Of those that a mesh axis runs over, the one named last changes fastest.
Arguments:
- feature_high: int32 [20, 2048], P(None, 'dp'), may hold values from 0 to 2047
- feature_low: int32 [20, 2048], P(None, 'dp'), may hold values from 0 to 2047
- labels: int32 [2048], P('dp'), may hold values 0 or 1
- weights: float32 [4194304], P(('dp', 'table')), may hold values from -0.6 to 0.6
- history_steps: float32 [8, 4194304], P(None, ('dp', 'table')), may hold values from -46 to 46
- history_diffs: float32 [8, 4194304], P(None, ('dp', 'table')), may hold values from -198 to 198, as said below
Outputs:
- direction: float32 [4194304], P(('dp', 'table'))
The draws below stay inside these ranges and needn't reach their ends.
Inputs may be any that keep to these rules, and one draw needn't show every extreme that they name: Each entry of history_diffs has the sign of the matching entry of history_steps and 0.2 to 4.3 times its magnitude.
All inputs are finite; a program needn't handle non-finite values. No bound on the sum of `labels` on one device may be relied on, other than what follows from the above.
Results may differ from the reference program's by a relative error of at most 0.0001.
Values sent between devices are 32-bit elements; how exact they have to be, the bound alone decides.
A program may use at most 64 MiB of HBM per device.

```python
import jax
import jax.numpy as jnp

TABLE = 4194304
SLOTS = 20
HASHES = 4
MEM = 8
EX_DEV = 256
EXAMPLES = 2048


def feature_pair(key):
    base_key = jax.random.fold_in(key, 31)
    keys = jax.random.split(base_key, 9)
    dp_count = EXAMPLES // EX_DEV
    block_width = TABLE // (dp_count * 4)
    spread_count = max(1, block_width // 2053)
    tops = jax.random.randint(keys[0], (SLOTS, EXAMPLES), 1, 2049)
    raw_high = jax.random.randint(keys[1], (SLOTS, EXAMPLES), 0, tops)
    odd_mult = 2 * jax.random.randint(keys[2], (SLOTS, 1), 0, 1024) + 1
    offset = jax.random.randint(keys[3], (SLOTS, 1), 0, 2048)
    high = (raw_high * odd_mult + offset) % 2048
    low = jax.random.randint(keys[4], (SLOTS, EXAMPLES), 0, 2048)
    chosen_device = jax.random.randint(keys[5], (), 0, dp_count)
    target_block = jax.random.randint(keys[6], (), 0, dp_count * 4)
    example = jnp.arange(EXAMPLES, dtype=jnp.int32)[None, :]
    picked = jax.random.randint(keys[7], (1, EXAMPLES), 0, 2) == 1
    crowded = (example // EX_DEV == chosen_device) & picked
    slot_index = jnp.arange(SLOTS, dtype=jnp.int32)[:, None]
    block_start = target_block * block_width
    remainder = (block_start - high * 40503 % TABLE - slot_index * 1543) % TABLE
    first_low = (remainder + 2052) // 2053
    nudge = jax.random.randint(keys[8], (SLOTS, EXAMPLES), 0, spread_count)
    aimed = (first_low + nudge) % 2048
    low = jnp.where(crowded, aimed, low)
    return (high.astype(jnp.int32), low.astype(jnp.int32))


def draw_feature_high(key, part):
    return feature_pair(key)[0]


def draw_feature_low(key, part):
    return feature_pair(key)[1]


def history_pair(key):
    base_key = jax.random.fold_in(key, 77)
    first, second, third, fourth = jax.random.split(base_key, 4)
    spot = jnp.arange(TABLE, dtype=jnp.float32)[None, :] / (TABLE - 1)
    order = jax.random.permutation(fourth, MEM)
    top_row = order[:, None] == MEM - 1
    column = jnp.arange(TABLE, dtype=jnp.int32)[None, :]
    base = jnp.clip(jax.random.normal(first, (MEM, TABLE), jnp.float32), -4.0, 4.0)
    ramp = 1.0 + 2.0 * spot
    steps = base * ramp
    plant_up = top_row & (column == TABLE - 1)
    plant_down = top_row & (column == TABLE - 2)
    steps = jnp.where(plant_up, 46.0, jnp.where(plant_down, -46.0, steps))
    factor = jnp.exp(jax.random.uniform(second, (MEM, TABLE), jnp.float32, jnp.log(0.5), jnp.log(4.0)))
    factor = factor + 0.3 * jax.random.uniform(third, (MEM, TABLE), jnp.float32, -1.0, 1.0)
    factor = jnp.where(plant_up | plant_down, 4.3, factor)
    return (steps, steps * factor)


def draw_history_steps(key, part):
    return history_pair(key)[0]


def draw_history_diffs(key, part):
    return history_pair(key)[1]


def plant(result, own_key, smallest, top_value):
    extent = result.shape
    place = [jax.random.randint(jax.random.fold_in(own_key, axis), (), 0, extent[axis]) for axis in range(len(extent))]
    result = result.at[tuple(place)].set(smallest)
    longest = extent.index(max(extent))
    place[longest] = (place[longest] + 1) % extent[longest]
    return result.at[tuple(place)].set(top_value)


def block_scale(stream_key, extent, cuts, least, top_value):
    level = 1.0
    for position, parts in cuts:
        draws = jax.random.uniform(jax.random.fold_in(jax.random.fold_in(stream_key, 6), position), (parts,), jnp.float32, least / len(cuts), top_value / len(cuts))
        level = level * jnp.repeat(jnp.exp(draws), extent[position] // parts).reshape((-1,) + (1,) * (len(extent) - 1 - position))
    return level


def bell_draw(own_key, dims, width, bound, cuts=(), kind=jnp.bfloat16):
    gain = block_scale(own_key, dims, cuts, -0.22, 0.18) if cuts else 1.0
    result = jax.random.normal(own_key, dims, jnp.float32) * width * gain
    return jnp.minimum(jnp.maximum(result, -bound), bound).astype(kind)


def setup_inputs(seed: int = 0) -> dict:
    seeds = jax.random.split(jax.random.key(seed), 7)
    return {
        "feature_high": draw_feature_high(jax.random.fold_in(seeds[6], 71), 0),
        "feature_low": draw_feature_low(jax.random.fold_in(seeds[6], 71), 0),
        "labels": plant((jax.random.randint(seeds[2], (EXAMPLES,), 0, 4) < 1).astype(jnp.int32), jax.random.fold_in(seeds[2], 1), 0, 1),
        "weights": bell_draw(seeds[3], (TABLE,), 0.1, 0.6, ((0, 32),), jnp.float32),
        "history_steps": draw_history_steps(jax.random.fold_in(seeds[6], 71), 0),
        "history_diffs": draw_history_diffs(jax.random.fold_in(seeds[6], 71), 0),
    }


high_mult = (40503, 96469, 255361, 362443)
low_mult = (2053, 6151, 12289, 98317)
slot_mult = (1543, 3079, 769, 3457)
shifts = (0, 1048573, 2097143, 3145727)
l2_weight = 1.0


def hashed(feature_high, feature_low, number):
    slot_index = jnp.arange(feature_high.shape[0], dtype=jnp.int32)[:, None]
    part_high = (feature_high * high_mult[number]) % TABLE
    part_low = (feature_low * low_mult[number]) % TABLE
    return ((part_high + part_low + slot_index * slot_mult[number] + shifts[number]) % TABLE).astype(jnp.int32)


def reference(feature_high, feature_low, labels, weights, history_steps, history_diffs):
    margin = jnp.zeros((feature_high.shape[1],), jnp.float32)
    for number in range(HASHES):
        indices = hashed(feature_high, feature_low, number)
        margin = margin + jnp.sum(weights[indices], axis=0)
    residual = jax.nn.sigmoid(margin) - labels.astype(jnp.float32)
    gradient = jnp.zeros((TABLE,), jnp.float32)
    for number in range(HASHES):
        indices = hashed(feature_high, feature_low, number)
        spread = jnp.broadcast_to(residual[None, :], indices.shape)
        gradient = gradient.at[indices.reshape(-1)].add(spread.reshape(-1))
    gradient = gradient + l2_weight * weights
    inverse = [1.0 / jnp.sum(history_steps[which] * history_diffs[which]) for which in range(MEM)]
    current = gradient
    alphas = [None] * MEM
    for which in reversed(range(MEM)):
        alphas[which] = inverse[which] * jnp.sum(history_steps[which] * current)
        current = current - alphas[which] * history_diffs[which]
    newest = MEM - 1
    scaling = jnp.sum(history_steps[newest] * history_diffs[newest]) / jnp.sum(history_diffs[newest] * history_diffs[newest])
    current = scaling * current
    for which in range(MEM):
        correction = inverse[which] * jnp.sum(history_diffs[which] * current)
        current = current + (alphas[which] - correction) * history_steps[which]
    return -current
```

```python
import functools

import jax
import jax.numpy as jnp
from jax import lax
from jax.experimental import pallas as pl
from jax.experimental.pallas import tpu as pltpu
from jax.sharding import PartitionSpec as P

HASHES = 4
LANES = 128
BLOCK = 16
GROUP = 4

high_mult = (40503, 96469, 255361, 362443)
low_mult = (2053, 6151, 12289, 98317)
slot_mult = (1543, 3079, 769, 3457)
shifts = (0, 1048573, 2097143, 3145727)
l2_weight = 1.0
F32, BF16, I32 = jnp.float32, jnp.bfloat16, jnp.int32


def iota(shape, axis):
    return lax.broadcasted_iota(I32, shape, axis)


def split(value):
    top = value.astype(BF16)
    return top, (value - top.astype(F32)).astype(BF16)


def hot(index, count):
    shape = (count, index.shape[1])
    return jnp.where(iota(shape, 0) == index, 1.0, 0.0).astype(BF16)


def gram_kernel(steps_ref, diffs_ref, out_ref, sums):
    @pl.when(pl.program_id(0) == 0)
    def _():
        sums[...] = jnp.zeros_like(sums)

    mem = steps_ref.shape[0]

    def body(number, carry):
        at = pl.ds(pl.multiple_of(number * LANES, LANES), LANES)
        step, diff = steps_ref[:, at], diffs_ref[:, at]
        new = []
        for i in range(mem):
            row = jnp.broadcast_to(diff[i : i + 1], diff.shape)
            new.append(carry[2 * i] + step * row)
            new.append(carry[2 * i + 1] + diff * row)
        return tuple(new)

    start = tuple(sums[i] for i in range(2 * mem))
    final = lax.fori_loop(0, steps_ref.shape[1] // LANES, body, start, unroll=4)
    for i in range(2 * mem):
        sums[i] = final[i]

    @pl.when(pl.program_id(0) == pl.num_programs(0) - 1)
    def _():
        lane = iota((mem, LANES), 1)
        total = jnp.zeros((mem, LANES), F32)
        for i in range(mem):
            for kind in range(2):
                column = jnp.sum(final[2 * i + kind], axis=1, keepdims=True)
                total = jnp.where(lane == kind * mem + i, column, total)
        out_ref[...] = total


def gram(steps, diffs):
    mem, width = steps.shape
    chunk = min(width, 16384)
    return pl.pallas_call(
        gram_kernel,
        grid=(width // chunk,),
        in_specs=[pl.BlockSpec((mem, chunk), lambda i: (0, i))] * 2,
        out_specs=pl.BlockSpec((mem, LANES), lambda i: (0, 0)),
        out_shape=jax.ShapeDtypeStruct((mem, LANES), F32),
        scratch_shapes=[pltpu.VMEM((2 * mem, mem, LANES), F32)],
        cost_estimate=pl.CostEstimate(flops=32 * mem * width, bytes_accessed=8 * mem * width, transcendentals=0),
        name="gram",
    )(steps, diffs)


def margin_kernel(count, subs, bits, high_ref, low_ref, weights_ref, margin_ref, slots_ref, levels_ref, table):
    device = lax.axis_index("dp") * lax.axis_size("table") + lax.axis_index("table")
    width = 1 << bits
    slot_total = high_ref.shape[0]
    tops, rests = split(weights_ref[...].T)
    table[: LANES] = tops
    table[LANES :] = rests

    def one_pass(number, _):
        base = number * BLOCK

        def body(slot, carry):
            seen, outs = carry[0], list(carry[1:])
            for sub in range(subs):
                group, half = sub // 2, sub % 2
                at = (slot, pl.ds(group * 8, 8), pl.ds(half * LANES, LANES))
                high, low = high_ref[at], low_ref[at]
                for k in range(HASHES):
                    index = (high * high_mult[k] + low * low_mult[k] + (slot * slot_mult[k] + shifts[k])) & (count - 1)
                    owned = (index >> bits) == device
                    place = jnp.where(owned, seen, -1)
                    code = (index & (width - 1)) | (sub << bits)
                    for level in range(BLOCK):
                        outs[level] = jnp.where(place == level, code, outs[level])
                    seen = seen + owned.astype(I32)
            return (seen, *outs)

        empty = jnp.full((8, LANES), -1, I32)
        final = lax.fori_loop(0, slot_total, body, (jnp.zeros((8, LANES), I32) - base,) + (empty,) * BLOCK)
        for level in range(BLOCK):
            slots_ref[:, base + level, :] = final[1 + level]
        return final[0] + base

    seen = one_pass(0, None)
    most = jnp.max(seen)
    lax.fori_loop(1, (most + BLOCK - 1) // BLOCK, lambda n, c: (one_pass(n, None), c)[1], 0)
    for row in range(8):
        levels_ref[row] = (jnp.max(seen[row : row + 1]) + GROUP - 1) // GROUP

    def rows(row, _):
        def body(number, total):
            codes = slots_ref[row, pl.ds(number * GROUP, GROUP), :]
            code = jnp.concatenate([codes[i : i + 1] for i in range(GROUP)], axis=1)
            local = code & (width - 1)
            found = jnp.dot(table[...], hot(local >> 7, width // LANES), preferred_element_type=F32)
            found = found[:LANES] + found[LANES:]
            chosen = jnp.where(iota(found.shape, 0) == (local & (LANES - 1)), found, 0.0)
            value = jnp.sum(chosen, axis=0, keepdims=True)
            sub = code >> bits
            for i in range(GROUP):
                at = slice(i * LANES, (i + 1) * LANES)
                total = total + jnp.where(iota((subs, LANES), 0) == sub[:, at], value[:, at], 0.0)
            return total

        margin_ref[row] = lax.fori_loop(0, levels_ref[row], body, jnp.zeros((subs, LANES), F32))
        return 0

    lax.fori_loop(0, 8, rows, 0)


def margins(high, low, weights, count, subs, bits):
    levels = -(-subs * HASHES * high.shape[0] // BLOCK) * BLOCK
    vmem = pl.BlockSpec(memory_space=pltpu.VMEM)
    return pl.pallas_call(
        functools.partial(margin_kernel, count, subs, bits),
        in_specs=[vmem] * 3,
        out_specs=[vmem, vmem, pl.BlockSpec(memory_space=pltpu.SMEM)],
        out_shape=[
            jax.ShapeDtypeStruct((8, subs, LANES), F32),
            jax.ShapeDtypeStruct((8, levels, LANES), I32),
            jax.ShapeDtypeStruct((8,), I32),
        ],
        scratch_shapes=[pltpu.VMEM((2 * LANES, (1 << bits) // LANES), BF16)],
        compiler_params=pltpu.CompilerParams(vmem_limit_bytes=40 << 20),
        name="margins",
    )(high, low, weights)


def gradient_kernel(subs, bits, margin_ref, labels_ref, slots_ref, levels_ref, weights_ref, steps_hbm, diffs_hbm,
                    gradient_ref, products_ref, residual, both, steps, diffs, sems):
    copies = [
        pltpu.make_async_copy(steps_hbm, steps, sems.at[0]),
        pltpu.make_async_copy(diffs_hbm, diffs, sems.at[1]),
    ]
    for copy in copies:
        copy.start()
    width = 1 << bits
    residual[...] = 1.0 / (1.0 + jnp.exp(-margin_ref[...])) - labels_ref[...].astype(F32)
    both[...] = jnp.zeros_like(both)

    def rows(row, _):
        value = residual[row]

        def body(number, _):
            codes = slots_ref[row, pl.ds(number * GROUP, GROUP), :]
            code = jnp.concatenate([codes[i : i + 1] for i in range(GROUP)], axis=1)
            local = code & (width - 1)
            sub = code >> bits
            wide = jnp.concatenate([value] * GROUP, axis=1)
            mine = jnp.sum(jnp.where(iota(wide.shape, 0) == sub, wide, 0.0), axis=0, keepdims=True)
            column = iota((LANES, GROUP * LANES), 0) == (local & (LANES - 1))
            top, rest = split(jnp.where(column, mine, 0.0))
            terms = jnp.concatenate([top, rest], axis=0)
            both[...] += lax.dot_general(
                hot(local >> 7, width // LANES), terms, (((1,), (1,)), ((), ())), preferred_element_type=F32
            )
            return 0

        lax.fori_loop(0, levels_ref[row], body, 0)
        return 0

    lax.fori_loop(0, 8, rows, 0)
    gradient_ref[...] = both[:, :LANES] + both[:, LANES:] + l2_weight * weights_ref[...]
    for copy in copies:
        copy.wait()
    mem = steps.shape[0]

    def body(number, carry):
        by_step, by_diff = carry
        tile = gradient_ref[pl.ds(pl.multiple_of(number * 8, 8), 8), :]
        for i in range(8):
            at = pl.ds(pl.multiple_of(number * 8 * LANES, LANES) + i * LANES, LANES)
            row = jnp.broadcast_to(tile[i : i + 1], (mem, LANES))
            by_step = by_step + steps[:, at] * row
            by_diff = by_diff + diffs[:, at] * row
        return by_step, by_diff

    zero = jnp.zeros((mem, LANES), F32)
    by_step, by_diff = lax.fori_loop(0, width // (8 * LANES), body, (zero, zero))
    lane = iota((mem, LANES), 1)
    products_ref[...] = jnp.where(
        lane == 0,
        jnp.sum(by_step, axis=1, keepdims=True),
        jnp.where(lane == 1, jnp.sum(by_diff, axis=1, keepdims=True), 0.0),
    )


def gradients(margin, labels, slots, levels, weights, steps, diffs, subs, bits):
    vmem = pl.BlockSpec(memory_space=pltpu.VMEM)
    hbm = pl.BlockSpec(memory_space=pl.ANY)
    mem, width = steps.shape
    return pl.pallas_call(
        functools.partial(gradient_kernel, subs, bits),
        in_specs=[vmem, vmem, vmem, pl.BlockSpec(memory_space=pltpu.SMEM), vmem, hbm, hbm],
        out_specs=[vmem, vmem],
        out_shape=[jax.ShapeDtypeStruct(weights.shape, F32), jax.ShapeDtypeStruct((mem, LANES), F32)],
        scratch_shapes=[
            pltpu.VMEM(margin.shape, F32),
            pltpu.VMEM((width // LANES, 2 * LANES), F32),
            pltpu.VMEM((mem, width), F32),
            pltpu.VMEM((mem, width), F32),
            pltpu.SemaphoreType.DMA((2,)),
        ],
        compiler_params=pltpu.CompilerParams(vmem_limit_bytes=40 << 20),
        name="gradient",
    )(margin, labels, slots, levels, weights, steps, diffs)


def coefficients(grams, products, mem):
    lane, place = iota((mem, LANES), 1), iota((mem, LANES), 0)

    def column(array, number):
        return jnp.broadcast_to(
            jnp.sum(jnp.where(lane == number, array, 0.0), axis=1, keepdims=True), (mem, LANES)
        )

    def pick(array, number):
        return jnp.broadcast_to(array[number : number + 1], (mem, LANES))

    cross = [column(grams, i) for i in range(mem)]
    square = [column(grams, mem + i) for i in range(mem)]
    pairs = [pick(cross[i], i) for i in range(mem)]
    inverse = [1.0 / pair for pair in pairs]
    by_step, by_diff = column(products, 0), column(products, 1)
    alphas = [None] * mem
    for i in reversed(range(mem)):
        alphas[i] = inverse[i] * pick(by_step, i)
        by_step = by_step - alphas[i] * cross[i]
        by_diff = by_diff - alphas[i] * square[i]
    scale = pairs[mem - 1] / pick(square[mem - 1], mem - 1)
    by_diff = scale * by_diff
    on_steps = jnp.zeros((mem, LANES), F32)
    on_diffs = jnp.zeros((mem, LANES), F32)
    for i in range(mem):
        extra = jnp.sum(on_steps * cross[i], axis=0, keepdims=True)
        beta = inverse[i] * (pick(by_diff, i) + extra)
        on_steps = jnp.where(place == i, alphas[i] - beta, on_steps)
        on_diffs = jnp.where(place == i, -scale * alphas[i], on_diffs)
    return scale, on_diffs, on_steps


def direction_kernel(grams_ref, products_ref, gradient_ref, steps_ref, diffs_ref, out_ref, factors):
    mem = steps_ref.shape[0]

    @pl.when(pl.program_id(0) == 0)
    def _():
        scale, on_diffs, on_steps = coefficients(grams_ref[...], products_ref[...], mem)
        factors[0], factors[1], factors[2] = -scale, -on_diffs, -on_steps

    scale, on_diffs, on_steps = factors[0], factors[1], factors[2]

    def body(number, _):
        rows = []
        for i in range(8):
            at = pl.ds(pl.multiple_of(number * 8 * LANES, LANES) + i * LANES, LANES)
            rows.append(jnp.sum(on_diffs * diffs_ref[:, at] + on_steps * steps_ref[:, at], axis=0, keepdims=True))
        at = pl.ds(pl.multiple_of(number * 8, 8), 8)
        out_ref[at, :] = scale * gradient_ref[at, :] + jnp.concatenate(rows, axis=0)
        return 0

    lax.fori_loop(0, out_ref.shape[0] // 8, body, 0, unroll=2)


def directions(grams, products, gradient, steps, diffs):
    mem, width = steps.shape
    chunk = min(width, 16384)
    whole = pl.BlockSpec((mem, LANES), lambda i: (0, 0))
    flat = pl.BlockSpec((chunk // LANES, LANES), lambda i: (i, 0))
    wide = pl.BlockSpec((mem, chunk), lambda i: (0, i))
    return pl.pallas_call(
        direction_kernel,
        grid=(width // chunk,),
        in_specs=[whole, whole, flat, wide, wide],
        out_specs=flat,
        out_shape=jax.ShapeDtypeStruct(gradient.shape, F32),
        scratch_shapes=[pltpu.VMEM((3, mem, LANES), F32)],
        name="direction",
    )(grams, products, gradient, steps, diffs)


def local(feature_high, feature_low, labels, weights, history_steps, history_diffs):
    width = weights.shape[0]
    parts = lax.axis_size("dp")
    count = width * parts * lax.axis_size("table")
    bits = width.bit_length() - 1
    slots = feature_high.shape[0]
    subs = parts * feature_high.shape[1] // 1024
    mine = jnp.concatenate([feature_high, feature_low, labels[None, :]], axis=0)
    every = lax.all_gather(mine, "dp", axis=1)
    high, low = every[:slots], every[slots : 2 * slots]
    label = every[2 * slots].reshape(parts // 8, 8, 2, LANES).transpose(1, 0, 2, 3).reshape(8, subs, LANES)
    table = weights.reshape(width // LANES, LANES)
    partial_gram = gram(history_steps, history_diffs)
    margin, listed, levels = margins(high, low, table, count, subs, bits)
    margin, grams = lax.psum((margin, partial_gram), ("dp", "table"))
    gradient, products = gradients(
        margin, label, listed, levels, table, history_steps, history_diffs, subs, bits
    )
    products = lax.psum(products, ("dp", "table"))
    return directions(grams, products, gradient, history_steps, history_diffs).reshape(-1)


def solution(mesh):
    placed = (
        P(None, "dp"),
        P(None, "dp"),
        P("dp"),
        P(("dp", "table")),
        P(None, ("dp", "table")),
        P(None, ("dp", "table")),
    )
    return jax.shard_map(
        local, mesh=mesh, in_specs=placed, out_specs=P(("dp", "table")), check_vma=False
    )
```

```python
import functools

import jax
import jax.numpy as jnp
from jax import lax
from jax.experimental import pallas as pl
from jax.experimental.pallas import tpu as pltpu
from jax.sharding import PartitionSpec as P

HASHES = 4
LANES = 128
BLOCK = 16
GROUP = 4

high_mult = (40503, 96469, 255361, 362443)
low_mult = (2053, 6151, 12289, 98317)
slot_mult = (1543, 3079, 769, 3457)
shifts = (0, 1048573, 2097143, 3145727)
l2_weight = 1.0
F32, BF16, I32 = jnp.float32, jnp.bfloat16, jnp.int32
MESH = pl.DeviceIdType.MESH
VMEM = pl.BlockSpec(memory_space=pltpu.VMEM)
HBM = pl.BlockSpec(memory_space=pltpu.HBM)
SMEM = pl.BlockSpec(memory_space=pltpu.SMEM)


def iota(shape, axis):
    return lax.broadcasted_iota(I32, shape, axis)


def split(value):
    top = value.astype(BF16)
    return top, (value - top.astype(F32)).astype(BF16)


def hot(index, count):
    shape = (count, index.shape[1])
    return jnp.where(iota(shape, 0) == index, 1.0, 0.0).astype(BF16)


def greet(peers):
    barrier = pltpu.get_barrier_semaphore()
    for peer in peers:
        pl.semaphore_signal(barrier, inc=1, device_id=peer, device_id_type=MESH)
    pl.semaphore_wait(barrier, len(peers))


def others(axis):
    size, me = lax.axis_size(axis), lax.axis_index(axis)
    return [{axis: lax.rem(me + step, size)} for step in range(1, size)]


def send(source, target, peers, send_sems, recv_sems):
    copies = []
    for number, peer in enumerate(peers):
        copy = pltpu.make_async_remote_copy(
            src_ref=source,
            dst_ref=target,
            send_sem=send_sems.at[number],
            recv_sem=recv_sems.at[number],
            device_id=peer,
            device_id_type=MESH,
        )
        copy.start()
        copies.append(copy)
    return copies


def all_sum(mine, near, far, near_sems, far_sems):
    total = mine
    for axis, held, sems in (("table", near, near_sems), ("dp", far, far_sems)):
        me = lax.axis_index(axis)
        held[me] = total
        for copy in send(held.at[me], held.at[me], others(axis), *sems):
            copy.wait()
        total = held[0]
        for number in range(1, held.shape[0]):
            total = total + held[number]
    return total


def sum_scratch(shape):
    near, far = lax.axis_size("table"), lax.axis_size("dp")
    return [
        pltpu.VMEM((near, *shape), F32),
        pltpu.VMEM((far, *shape), F32),
        pltpu.SemaphoreType.DMA((near - 1,)),
        pltpu.SemaphoreType.DMA((near - 1,)),
        pltpu.SemaphoreType.DMA((far - 1,)),
        pltpu.SemaphoreType.DMA((far - 1,)),
    ]


def share_kernel(high_ref, low_ref, labels_ref, steps_hbm, diffs_hbm, every_ref, gram_ref,
                 steps, diffs, send_sems, recv_sems, step_sems, diff_sems):
    mem, width = steps.shape
    slots = high_ref.shape[0]
    parts = step_sems.shape[0]
    copies = []
    for part in range(parts):
        at = (slice(None), pl.ds(part * (width // parts), width // parts))
        for source, target, sems in ((steps_hbm, steps, step_sems), (diffs_hbm, diffs, diff_sems)):
            copy = pltpu.make_async_copy(source.at[at], target.at[at], sems.at[part])
            copy.start()
            copies.append(copy)
    me = lax.axis_index("dp")
    every_ref[me, :slots] = high_ref[...]
    every_ref[me, slots : 2 * slots] = low_ref[...]
    every_ref[me, 2 * slots : 2 * slots + 1] = labels_ref[...]
    if every_ref.shape[1] > 2 * slots + 1:
        rest = every_ref.shape[1] - 2 * slots - 1
        every_ref[me, 2 * slots + 1 :] = jnp.zeros((rest, labels_ref.shape[1]), I32)
    peers = others("dp")
    greet(peers)
    sent = send(every_ref.at[me], every_ref.at[me], peers, send_sems, recv_sems)

    def body(number, carry):
        at = pl.ds(pl.multiple_of(number * LANES, LANES), LANES)
        step, diff = steps[:, at], diffs[:, at]
        new = []
        for i in range(mem):
            row = jnp.broadcast_to(diff[i : i + 1], diff.shape)
            new.append(carry[2 * i] + step * row)
            new.append(carry[2 * i + 1] + diff * row)
        return tuple(new)

    final = (jnp.zeros((mem, LANES), F32),) * (2 * mem)
    each = width // parts // LANES
    for part in range(parts):
        copies[2 * part].wait()
        copies[2 * part + 1].wait()
        final = lax.fori_loop(part * each, (part + 1) * each, body, final, unroll=4)
    lane = iota((mem, LANES), 1)
    total = jnp.zeros((mem, LANES), F32)
    for i in range(mem):
        for kind in range(2):
            column = jnp.sum(final[2 * i + kind], axis=1, keepdims=True)
            total = jnp.where(lane == kind * mem + i, column, total)
    gram_ref[...] = total
    for copy in sent:
        copy.wait()


def share(high, low, labels, steps, diffs):
    mem, width = steps.shape
    rows = -(-(2 * high.shape[0] + 1) // 8) * 8
    dp = lax.axis_size("dp")
    parts = 4
    return pl.pallas_call(
        share_kernel,
        in_specs=[VMEM] * 3 + [HBM] * 2,
        out_specs=[VMEM] * 2,
        out_shape=[
            jax.ShapeDtypeStruct((dp, rows, high.shape[1]), I32),
            jax.ShapeDtypeStruct((mem, LANES), F32),
        ],
        scratch_shapes=[
            pltpu.VMEM((mem, width), F32),
            pltpu.VMEM((mem, width), F32),
            pltpu.SemaphoreType.DMA((dp - 1,)),
            pltpu.SemaphoreType.DMA((dp - 1,)),
            pltpu.SemaphoreType.DMA((parts,)),
            pltpu.SemaphoreType.DMA((parts,)),
        ],
        compiler_params=pltpu.CompilerParams(
            vmem_limit_bytes=40 << 20, collective_id=0, has_side_effects=True
        ),
        name="share",
    )(high, low, labels.reshape(1, -1), steps, diffs)


def reduce_kernel(margin_ref, gram_ref, out_ref, own, near, far, *sems):
    subs = margin_ref.shape[0]
    greet(others("table") + others("dp"))
    own[:subs] = margin_ref[...]
    own[subs] = gram_ref[...]
    out_ref[...] = all_sum(own[...], near, far, sems[:2], sems[2:])


def reduced(margin, grams):
    shape = (margin.shape[0] + 1, *margin.shape[1:])
    return pl.pallas_call(
        reduce_kernel,
        in_specs=[VMEM] * 2,
        out_specs=VMEM,
        out_shape=jax.ShapeDtypeStruct(shape, F32),
        scratch_shapes=[pltpu.VMEM(shape, F32)] + sum_scratch(shape),
        compiler_params=pltpu.CompilerParams(collective_id=1, has_side_effects=True),
        name="reduce",
    )(margin, grams)


def margin_kernel(count, subs, bits, slot_total, every_ref, weights_ref, margin_ref, slots_ref, levels_ref, table, features):
    device = lax.axis_index("dp") * lax.axis_size("table") + lax.axis_index("table")
    width = 1 << bits
    for number in range(2 * slot_total):
        features[number] = every_ref[:, number, :]
    tops, rests = split(weights_ref[...].T)
    table[: LANES] = tops
    table[LANES :] = rests

    def one_pass(number, _):
        base = number * BLOCK

        def body(slot, carry):
            seen, outs = carry[0], list(carry[1:])
            for sub in range(subs):
                group, half = sub // 2, sub % 2
                at = (pl.ds(group * 8, 8), pl.ds(half * LANES, LANES))
                high, low = features[(slot, *at)], features[(slot + slot_total, *at)]
                for k in range(HASHES):
                    index = (high * high_mult[k] + low * low_mult[k] + (slot * slot_mult[k] + shifts[k])) & (count - 1)
                    owned = (index >> bits) == device
                    place = jnp.where(owned, seen, -1)
                    code = (index & (width - 1)) | (sub << bits)
                    for level in range(BLOCK):
                        outs[level] = jnp.where(place == level, code, outs[level])
                    seen = seen + owned.astype(I32)
            return (seen, *outs)

        empty = jnp.full((8, LANES), -1, I32)
        final = lax.fori_loop(0, slot_total, body, (jnp.zeros((8, LANES), I32) - base,) + (empty,) * BLOCK)
        for level in range(BLOCK):
            slots_ref[:, base + level, :] = final[1 + level]
        return final[0] + base

    seen = one_pass(0, None)
    most = jnp.max(seen)
    lax.fori_loop(1, (most + BLOCK - 1) // BLOCK, lambda n, c: (one_pass(n, None), c)[1], 0)
    for row in range(8):
        levels_ref[row] = (jnp.max(seen[row : row + 1]) + GROUP - 1) // GROUP

    def rows(row, _):
        def body(number, total):
            codes = slots_ref[row, pl.ds(number * GROUP, GROUP), :]
            code = jnp.concatenate([codes[i : i + 1] for i in range(GROUP)], axis=1)
            local = code & (width - 1)
            found = jnp.dot(table[...], hot(local >> 7, width // LANES), preferred_element_type=F32)
            found = found[:LANES] + found[LANES:]
            chosen = jnp.where(iota(found.shape, 0) == (local & (LANES - 1)), found, 0.0)
            value = jnp.sum(chosen, axis=0, keepdims=True)
            sub = code >> bits
            for i in range(GROUP):
                at = slice(i * LANES, (i + 1) * LANES)
                total = total + jnp.where(iota((subs, LANES), 0) == sub[:, at], value[:, at], 0.0)
            return total

        total = lax.fori_loop(0, levels_ref[row], body, jnp.zeros((subs, LANES), F32))
        for sub in range(subs):
            here = iota((8, LANES), 0) == row
            margin_ref[sub] = jnp.where(here, total[sub : sub + 1], margin_ref[sub])
        return 0

    margin_ref[...] = jnp.zeros_like(margin_ref)
    lax.fori_loop(0, 8, rows, 0)


def margins(every, weights, count, subs, bits, slots):
    levels = -(-subs * HASHES * slots // BLOCK) * BLOCK
    return pl.pallas_call(
        functools.partial(margin_kernel, count, subs, bits, slots),
        in_specs=[VMEM] * 2,
        out_specs=[VMEM, VMEM, SMEM],
        out_shape=[
            jax.ShapeDtypeStruct((subs, 8, LANES), F32),
            jax.ShapeDtypeStruct((8, levels, LANES), I32),
            jax.ShapeDtypeStruct((8,), I32),
        ],
        scratch_shapes=[
            pltpu.VMEM((2 * LANES, (1 << bits) // LANES), BF16),
            pltpu.VMEM((2 * slots, every.shape[0], every.shape[2]), I32),
        ],
        compiler_params=pltpu.CompilerParams(vmem_limit_bytes=40 << 20),
        name="margins",
    )(every, weights)


def gradient_kernel(subs, bits, label_row, total_ref, every_ref, slots_ref, levels_ref, weights_ref, steps_hbm, diffs_hbm,
                    gradient_ref, products_ref, residual, both, steps, diffs, sems):
    copies = [
        pltpu.make_async_copy(steps_hbm, steps, sems.at[0]),
        pltpu.make_async_copy(diffs_hbm, diffs, sems.at[1]),
    ]
    for copy in copies:
        copy.start()
    width = 1 << bits
    for sub in range(subs):
        label = every_ref[sub // 2 * 8 : sub // 2 * 8 + 8, label_row, sub % 2 * LANES : sub % 2 * LANES + LANES]
        residual[:, sub, :] = 1.0 / (1.0 + jnp.exp(-total_ref[sub])) - label.astype(F32)
    both[...] = jnp.zeros_like(both)

    def rows(row, _):
        value = residual[row]

        def body(number, _):
            codes = slots_ref[row, pl.ds(number * GROUP, GROUP), :]
            code = jnp.concatenate([codes[i : i + 1] for i in range(GROUP)], axis=1)
            local = code & (width - 1)
            sub = code >> bits
            wide = jnp.concatenate([value] * GROUP, axis=1)
            mine = jnp.sum(jnp.where(iota(wide.shape, 0) == sub, wide, 0.0), axis=0, keepdims=True)
            column = iota((LANES, GROUP * LANES), 0) == (local & (LANES - 1))
            top, rest = split(jnp.where(column, mine, 0.0))
            terms = jnp.concatenate([top, rest], axis=0)
            both[...] += lax.dot_general(
                hot(local >> 7, width // LANES), terms, (((1,), (1,)), ((), ())), preferred_element_type=F32
            )
            return 0

        lax.fori_loop(0, levels_ref[row], body, 0)
        return 0

    lax.fori_loop(0, 8, rows, 0)
    gradient_ref[...] = both[:, :LANES] + both[:, LANES:] + l2_weight * weights_ref[...]
    for copy in copies:
        copy.wait()
    mem = steps.shape[0]

    def body(number, carry):
        by_step, by_diff = carry
        tile = gradient_ref[pl.ds(pl.multiple_of(number * 8, 8), 8), :]
        for i in range(8):
            at = pl.ds(pl.multiple_of(number * 8 * LANES, LANES) + i * LANES, LANES)
            row = jnp.broadcast_to(tile[i : i + 1], (mem, LANES))
            by_step = by_step + steps[:, at] * row
            by_diff = by_diff + diffs[:, at] * row
        return by_step, by_diff

    zero = jnp.zeros((mem, LANES), F32)
    by_step, by_diff = lax.fori_loop(0, width // (8 * LANES), body, (zero, zero))
    lane = iota((mem, LANES), 1)
    products_ref[...] = jnp.where(
        lane == 0,
        jnp.sum(by_step, axis=1, keepdims=True),
        jnp.where(lane == 1, jnp.sum(by_diff, axis=1, keepdims=True), 0.0),
    )


def gradients(total, every, slots, levels, weights, steps, diffs, subs, bits, label_row):
    mem, width = steps.shape
    return pl.pallas_call(
        functools.partial(gradient_kernel, subs, bits, label_row),
        in_specs=[VMEM, VMEM, VMEM, SMEM, VMEM, HBM, HBM],
        out_specs=[VMEM, VMEM],
        out_shape=[jax.ShapeDtypeStruct(weights.shape, F32), jax.ShapeDtypeStruct((mem, LANES), F32)],
        scratch_shapes=[
            pltpu.VMEM((8, subs, LANES), F32),
            pltpu.VMEM((width // LANES, 2 * LANES), F32),
            pltpu.VMEM((mem, width), F32),
            pltpu.VMEM((mem, width), F32),
            pltpu.SemaphoreType.DMA((2,)),
        ],
        compiler_params=pltpu.CompilerParams(vmem_limit_bytes=40 << 20),
        name="gradient",
    )(total, every, slots, levels, weights, steps, diffs)


def coefficients(grams, products, mem):
    lane, place = iota((mem, LANES), 1), iota((mem, LANES), 0)

    def column(array, number):
        return jnp.broadcast_to(
            jnp.sum(jnp.where(lane == number, array, 0.0), axis=1, keepdims=True), (mem, LANES)
        )

    def pick(array, number):
        return jnp.broadcast_to(array[number : number + 1], (mem, LANES))

    cross = [column(grams, i) for i in range(mem)]
    square = [column(grams, mem + i) for i in range(mem)]
    pairs = [pick(cross[i], i) for i in range(mem)]
    inverse = [1.0 / pair for pair in pairs]
    by_step, by_diff = column(products, 0), column(products, 1)
    alphas = [None] * mem
    for i in reversed(range(mem)):
        alphas[i] = inverse[i] * pick(by_step, i)
        by_step = by_step - alphas[i] * cross[i]
        by_diff = by_diff - alphas[i] * square[i]
    scale = pairs[mem - 1] / pick(square[mem - 1], mem - 1)
    by_diff = scale * by_diff
    on_steps = jnp.zeros((mem, LANES), F32)
    on_diffs = jnp.zeros((mem, LANES), F32)
    for i in range(mem):
        extra = jnp.sum(on_steps * cross[i], axis=0, keepdims=True)
        beta = inverse[i] * (pick(by_diff, i) + extra)
        on_steps = jnp.where(place == i, alphas[i] - beta, on_steps)
        on_diffs = jnp.where(place == i, -scale * alphas[i], on_diffs)
    return scale, on_diffs, on_steps


def direction_kernel(total_ref, products_ref, gradient_ref, steps_hbm, diffs_hbm, out_ref,
                     steps, diffs, local_sems, near, far, *sems):
    mem = steps.shape[0]
    copies = [
        pltpu.make_async_copy(steps_hbm, steps, local_sems.at[0]),
        pltpu.make_async_copy(diffs_hbm, diffs, local_sems.at[1]),
    ]
    for copy in copies:
        copy.start()
    greet(others("table") + others("dp"))
    products = all_sum(products_ref[...], near, far, sems[:2], sems[2:])
    scale, on_diffs, on_steps = coefficients(total_ref[total_ref.shape[0] - 1], products, mem)
    scale, on_diffs, on_steps = -scale, -on_diffs, -on_steps
    for copy in copies:
        copy.wait()

    def body(number, _):
        rows = []
        for i in range(8):
            at = pl.ds(pl.multiple_of(number * 8 * LANES, LANES) + i * LANES, LANES)
            rows.append(jnp.sum(on_diffs * diffs[:, at] + on_steps * steps[:, at], axis=0, keepdims=True))
        at = pl.ds(pl.multiple_of(number * 8, 8), 8)
        out_ref[at, :] = scale * gradient_ref[at, :] + jnp.concatenate(rows, axis=0)
        return 0

    lax.fori_loop(0, out_ref.shape[0] // 8, body, 0, unroll=2)


def directions(total, products, gradient, steps, diffs):
    mem, width = steps.shape
    return pl.pallas_call(
        direction_kernel,
        in_specs=[VMEM] * 3 + [HBM] * 2,
        out_specs=VMEM,
        out_shape=jax.ShapeDtypeStruct(gradient.shape, F32),
        scratch_shapes=[
            pltpu.VMEM((mem, width), F32),
            pltpu.VMEM((mem, width), F32),
            pltpu.SemaphoreType.DMA((2,)),
        ]
        + sum_scratch((mem, LANES)),
        compiler_params=pltpu.CompilerParams(
            vmem_limit_bytes=40 << 20, collective_id=2, has_side_effects=True
        ),
        name="direction",
    )(total, products, gradient, steps, diffs)


def local(feature_high, feature_low, labels, weights, history_steps, history_diffs):
    width = weights.shape[0]
    parts = lax.axis_size("dp")
    count = width * parts * lax.axis_size("table")
    bits = width.bit_length() - 1
    slots = feature_high.shape[0]
    subs = parts * feature_high.shape[1] // 1024
    table = weights.reshape(width // LANES, LANES)
    every, partial_gram = share(feature_high, feature_low, labels, history_steps, history_diffs)
    margin, listed, levels = margins(every, table, count, subs, bits, slots)
    total = reduced(margin, partial_gram)
    gradient, products = gradients(
        total, every, listed, levels, table, history_steps, history_diffs, subs, bits, 2 * slots
    )
    return directions(total, products, gradient, history_steps, history_diffs).reshape(-1)


def solution(mesh):
    placed = (
        P(None, "dp"),
        P(None, "dp"),
        P("dp"),
        P(("dp", "table")),
        P(None, ("dp", "table")),
        P(None, ("dp", "table")),
    )
    return jax.shard_map(
        local, mesh=mesh, in_specs=placed, out_specs=P(("dp", "table")), check_vma=False
    )
```

```python
import functools

import jax
import jax.numpy as jnp
from jax import lax
from jax.experimental import pallas as pl
from jax.experimental.pallas import tpu as pltpu
from jax.sharding import PartitionSpec as P

HASHES = 4
LANES = 128
BLOCK = 16
GROUP = 4

high_mult = (40503, 96469, 255361, 362443)
low_mult = (2053, 6151, 12289, 98317)
slot_mult = (1543, 3079, 769, 3457)
shifts = (0, 1048573, 2097143, 3145727)
l2_weight = 1.0
BUDGET = 60 << 20
F32, BF16, I32 = jnp.float32, jnp.bfloat16, jnp.int32
MESH = pl.DeviceIdType.MESH
VMEM = pl.BlockSpec(memory_space=pltpu.VMEM)
HBM = pl.BlockSpec(memory_space=pltpu.HBM)
SMEM = pl.BlockSpec(memory_space=pltpu.SMEM)


def iota(shape, axis):
    return lax.broadcasted_iota(I32, shape, axis)


def split(value):
    top = value.astype(BF16)
    return top, (value - top.astype(F32)).astype(BF16)


def hot(index, count):
    shape = (count, index.shape[1])
    return jnp.where(iota(shape, 0) == index, 1.0, 0.0).astype(BF16)


def greet(peers):
    barrier = pltpu.get_barrier_semaphore()
    for peer in peers:
        pl.semaphore_signal(barrier, inc=1, device_id=peer, device_id_type=MESH)
    pl.semaphore_wait(barrier, len(peers))


def others(axis):
    size, me = lax.axis_size(axis), lax.axis_index(axis)
    return [{axis: lax.rem(me + step, size)} for step in range(1, size)]


def send(source, target, peers, send_sems, recv_sems):
    copies = []
    for number, peer in enumerate(peers):
        copy = pltpu.make_async_remote_copy(
            src_ref=source,
            dst_ref=target,
            send_sem=send_sems.at[number],
            recv_sem=recv_sems.at[number],
            device_id=peer,
            device_id_type=MESH,
        )
        copy.start()
        copies.append(copy)
    return copies


def stage(axis, held, value, sems):
    me = lax.axis_index(axis)
    held[me] = value
    return send(held.at[me], held.at[me], others(axis), *sems)


def finish(copies, held):
    for copy in copies:
        copy.wait()
    total = held[0]
    for number in range(1, held.shape[0]):
        total = total + held[number]
    return total


def sum_scratch(shape):
    near, far = lax.axis_size("table"), lax.axis_size("dp")
    return [
        pltpu.VMEM((near, *shape), F32),
        pltpu.VMEM((far, *shape), F32),
        pltpu.SemaphoreType.DMA((near - 1,)),
        pltpu.SemaphoreType.DMA((near - 1,)),
        pltpu.SemaphoreType.DMA((far - 1,)),
        pltpu.SemaphoreType.DMA((far - 1,)),
    ]


def load(steps_hbm, diffs_hbm, steps, diffs, sems, first=0):
    parts, width = sems.shape[1], steps.shape[1]
    pairs = []
    for part in range(parts):
        size = width // parts
        pair = []
        for kind, (source, target) in enumerate(((steps_hbm, steps), (diffs_hbm, diffs))):
            copy = pltpu.make_async_copy(
                source.at[:, pl.ds(first + part * size, size)],
                target.at[:, pl.ds(part * size, size)],
                sems.at[kind, part],
            )
            copy.start()
            pair.append(copy)
        pairs.append(pair)
    return pairs


def gram_part(steps, diffs, pairs, part, carry):
    mem = steps.shape[0]
    each = steps.shape[1] // len(pairs) // LANES
    for copy in pairs[part]:
        copy.wait()

    def body(number, carry):
        at = pl.ds(pl.multiple_of(number * LANES, LANES), LANES)
        step, diff = steps[:, at], diffs[:, at]
        new = []
        for i in range(mem):
            row = jnp.broadcast_to(diffs[i : i + 1, at], diff.shape)
            new.append(carry[2 * i] + step * row)
            new.append(carry[2 * i + 1] + diff * row)
        return tuple(new)

    return lax.fori_loop(part * each, (part + 1) * each, body, carry, unroll=4)


def to_row(columns):
    mem = columns[0].shape[0]
    total = jnp.zeros((mem, LANES), F32)
    spot = iota((mem, LANES), 1) - iota((mem, LANES), 0)
    for number, column in enumerate(columns):
        total = jnp.where(spot == number * mem, jnp.sum(column, axis=1, keepdims=True), total)
    return jnp.sum(total, axis=0, keepdims=True)


def from_row(row, number, mem):
    spot = iota((mem, LANES), 1) - iota((mem, LANES), 0)
    wide = jnp.broadcast_to(row, (mem, LANES))
    column = jnp.sum(jnp.where(spot == number * mem, wide, 0.0), axis=1, keepdims=True)
    return jnp.broadcast_to(column, (mem, LANES))


def gram_row(carry, mem):
    return to_row([carry[2 * i] for i in range(mem)] + [carry[2 * i + 1] for i in range(mem)])


def share_kernel(high_ref, low_ref, labels_ref, steps_hbm, diffs_hbm, every_ref, gram_ref,
                 steps, diffs, send_sems, recv_sems, sems):
    mem = steps.shape[0]
    slots = high_ref.shape[0]
    pairs = load(steps_hbm, diffs_hbm, steps, diffs, sems)
    me = lax.axis_index("dp")
    every_ref[me, :slots] = high_ref[...]
    every_ref[me, slots : 2 * slots] = low_ref[...]
    every_ref[me, 2 * slots : 2 * slots + 1] = labels_ref[...]
    if every_ref.shape[1] > 2 * slots + 1:
        rest = every_ref.shape[1] - 2 * slots - 1
        every_ref[me, 2 * slots + 1 :] = jnp.zeros((rest, labels_ref.shape[1]), I32)
    peers = others("dp")
    greet(peers)
    sent = send(every_ref.at[me], every_ref.at[me], peers, send_sems, recv_sems)
    carry = (jnp.zeros((mem, LANES), F32),) * (2 * mem)
    for part in range(len(pairs)):
        carry = gram_part(steps, diffs, pairs, part, carry)
    gram_ref[...] = gram_row(carry, mem)
    for copy in sent:
        copy.wait()


def share(high, low, labels, steps, diffs):
    mem, width = steps.shape
    rows = -(-(2 * high.shape[0] + 1) // 8) * 8
    dp = lax.axis_size("dp")
    return pl.pallas_call(
        share_kernel,
        in_specs=[VMEM] * 3 + [HBM] * 2,
        out_specs=[VMEM] * 2,
        out_shape=[
            jax.ShapeDtypeStruct((dp, rows, high.shape[1]), I32),
            jax.ShapeDtypeStruct((1, LANES), F32),
        ],
        scratch_shapes=[
            pltpu.VMEM((mem, width // 2), F32),
            pltpu.VMEM((mem, width // 2), F32),
            pltpu.SemaphoreType.DMA((dp - 1,)),
            pltpu.SemaphoreType.DMA((dp - 1,)),
            pltpu.SemaphoreType.DMA((2, 2)),
        ],
        compiler_params=pltpu.CompilerParams(
            vmem_limit_bytes=BUDGET, collective_id=0, has_side_effects=True
        ),
        name="share",
    )(high, low, labels.reshape(1, -1), steps, diffs)


def reduce_kernel(margin_ref, gram_ref, steps_hbm, diffs_hbm, out_ref, grams_ref,
                  steps, diffs, load_sems, near, far, *sems):
    mem, half = steps.shape
    pairs = load(steps_hbm, diffs_hbm, steps, diffs, load_sems, half)
    greet(others("table") + others("dp"))
    carry = (jnp.zeros((mem, LANES), F32),) * (2 * mem)
    copies = stage("table", near, margin_ref[...], sems[:2])
    carry = gram_part(steps, diffs, pairs, 0, carry)
    copies = stage("dp", far, finish(copies, near), sems[2:])
    carry = gram_part(steps, diffs, pairs, 1, carry)
    grams_ref[...] = gram_ref[...] + gram_row(carry, mem)
    out_ref[...] = finish(copies, far)


def reduced(margin, grams, steps, diffs):
    mem, width = steps.shape
    return pl.pallas_call(
        reduce_kernel,
        in_specs=[VMEM] * 2 + [HBM] * 2,
        out_specs=[VMEM] * 2,
        out_shape=[
            jax.ShapeDtypeStruct(margin.shape, F32),
            jax.ShapeDtypeStruct((1, LANES), F32),
        ],
        scratch_shapes=[
            pltpu.VMEM((mem, width // 2), F32),
            pltpu.VMEM((mem, width // 2), F32),
            pltpu.SemaphoreType.DMA((2, 2)),
        ]
        + sum_scratch(margin.shape),
        compiler_params=pltpu.CompilerParams(
            vmem_limit_bytes=BUDGET, collective_id=1, has_side_effects=True
        ),
        name="reduce",
    )(margin, grams, steps, diffs)


def margin_kernel(count, subs, bits, slot_total, every_ref, weights_ref, margin_ref, slots_ref, levels_ref, table, features):
    device = lax.axis_index("dp") * lax.axis_size("table") + lax.axis_index("table")
    width = 1 << bits
    for number in range(2 * slot_total):
        features[number] = every_ref[:, number, :]
    tops, rests = split(weights_ref[...].T)
    table[: LANES] = tops
    table[LANES :] = rests

    def one_pass(number, _):
        base = number * BLOCK

        def body(slot, carry):
            seen, outs = carry[0], list(carry[1:])
            for sub in range(subs):
                group, half = sub // 2, sub % 2
                at = (pl.ds(group * 8, 8), pl.ds(half * LANES, LANES))
                high, low = features[(slot, *at)], features[(slot + slot_total, *at)]
                for k in range(HASHES):
                    index = (high * high_mult[k] + low * low_mult[k] + (slot * slot_mult[k] + shifts[k])) & (count - 1)
                    owned = (index >> bits) == device
                    place = jnp.where(owned, seen, -1)
                    code = (index & (width - 1)) | (sub << bits)
                    for level in range(BLOCK):
                        outs[level] = jnp.where(place == level, code, outs[level])
                    seen = seen + owned.astype(I32)
            return (seen, *outs)

        empty = jnp.full((8, LANES), -1, I32)
        final = lax.fori_loop(0, slot_total, body, (jnp.zeros((8, LANES), I32) - base,) + (empty,) * BLOCK)
        for level in range(BLOCK):
            slots_ref[:, base + level, :] = final[1 + level]
        return final[0] + base

    seen = one_pass(0, None)
    most = jnp.max(seen)
    lax.fori_loop(1, (most + BLOCK - 1) // BLOCK, lambda n, c: (one_pass(n, None), c)[1], 0)
    for row in range(8):
        levels_ref[row] = (jnp.max(seen[row : row + 1]) + GROUP - 1) // GROUP

    def rows(row, _):
        def body(number, total):
            codes = slots_ref[row, pl.ds(number * GROUP, GROUP), :]
            code = jnp.concatenate([codes[i : i + 1] for i in range(GROUP)], axis=1)
            local = code & (width - 1)
            found = jnp.dot(table[...], hot(local >> 7, width // LANES), preferred_element_type=F32)
            found = found[:LANES] + found[LANES:]
            chosen = jnp.where(iota(found.shape, 0) == (local & (LANES - 1)), found, 0.0)
            value = jnp.sum(chosen, axis=0, keepdims=True)
            sub = code >> bits
            for i in range(GROUP):
                at = slice(i * LANES, (i + 1) * LANES)
                total = total + jnp.where(iota((subs, LANES), 0) == sub[:, at], value[:, at], 0.0)
            return total

        total = lax.fori_loop(0, levels_ref[row], body, jnp.zeros((subs, LANES), F32))
        for sub in range(subs):
            here = iota((8, LANES), 0) == row
            margin_ref[sub] = jnp.where(here, total[sub : sub + 1], margin_ref[sub])
        return 0

    margin_ref[...] = jnp.zeros_like(margin_ref)
    lax.fori_loop(0, 8, rows, 0)


def margins(every, weights, count, subs, bits, slots):
    levels = -(-subs * HASHES * slots // BLOCK) * BLOCK
    return pl.pallas_call(
        functools.partial(margin_kernel, count, subs, bits, slots),
        in_specs=[VMEM] * 2,
        out_specs=[VMEM, VMEM, SMEM],
        out_shape=[
            jax.ShapeDtypeStruct((subs, 8, LANES), F32),
            jax.ShapeDtypeStruct((8, levels, LANES), I32),
            jax.ShapeDtypeStruct((8,), I32),
        ],
        scratch_shapes=[
            pltpu.VMEM((2 * LANES, (1 << bits) // LANES), BF16),
            pltpu.VMEM((2 * slots, every.shape[0], every.shape[2]), I32),
        ],
        compiler_params=pltpu.CompilerParams(vmem_limit_bytes=BUDGET),
        name="margins",
    )(every, weights)


def gradient_kernel(subs, bits, label_row, total_ref, every_ref, slots_ref, levels_ref, weights_ref,
                    gradient_ref, residual, both):
    width = 1 << bits
    for sub in range(subs):
        label = every_ref[sub // 2 * 8 : sub // 2 * 8 + 8, label_row, sub % 2 * LANES : sub % 2 * LANES + LANES]
        residual[:, sub, :] = 1.0 / (1.0 + jnp.exp(-total_ref[sub])) - label.astype(F32)
    both[...] = jnp.zeros_like(both)

    def rows(row, _):
        value = residual[row]

        def body(number, _):
            codes = slots_ref[row, pl.ds(number * GROUP, GROUP), :]
            code = jnp.concatenate([codes[i : i + 1] for i in range(GROUP)], axis=1)
            local = code & (width - 1)
            sub = code >> bits
            wide = jnp.concatenate([value] * GROUP, axis=1)
            mine = jnp.sum(jnp.where(iota(wide.shape, 0) == sub, wide, 0.0), axis=0, keepdims=True)
            column = iota((LANES, GROUP * LANES), 0) == (local & (LANES - 1))
            top, rest = split(jnp.where(column, mine, 0.0))
            terms = jnp.concatenate([top, rest], axis=0)
            both[...] += lax.dot_general(
                hot(local >> 7, width // LANES), terms, (((1,), (1,)), ((), ())), preferred_element_type=F32
            )
            return 0

        lax.fori_loop(0, levels_ref[row], body, 0)
        return 0

    lax.fori_loop(0, 8, rows, 0)
    gradient_ref[...] = both[:, :LANES] + both[:, LANES:] + l2_weight * weights_ref[...]


def gradients(total, every, slots, levels, weights, subs, bits, label_row):
    return pl.pallas_call(
        functools.partial(gradient_kernel, subs, bits, label_row),
        in_specs=[VMEM, VMEM, VMEM, SMEM, VMEM],
        out_specs=VMEM,
        out_shape=jax.ShapeDtypeStruct(weights.shape, F32),
        scratch_shapes=[
            pltpu.VMEM((8, subs, LANES), F32),
            pltpu.VMEM((weights.shape[0], 2 * LANES), F32),
        ],
        compiler_params=pltpu.CompilerParams(vmem_limit_bytes=BUDGET),
        name="gradient",
    )(total, every, slots, levels, weights)


def coefficients(grams, products, mem):
    place = iota((mem, LANES), 0)

    def pick(array, number):
        return jnp.broadcast_to(array[number : number + 1], (mem, LANES))

    cross = [from_row(grams, i, mem) for i in range(mem)]
    square = [from_row(grams, mem + i, mem) for i in range(mem)]
    pairs = [pick(cross[i], i) for i in range(mem)]
    inverse = [1.0 / pair for pair in pairs]
    by_step, by_diff = from_row(products, 0, mem), from_row(products, 1, mem)
    alphas = [None] * mem
    for i in reversed(range(mem)):
        alphas[i] = inverse[i] * pick(by_step, i)
        by_step = by_step - alphas[i] * cross[i]
        by_diff = by_diff - alphas[i] * square[i]
    scale = pairs[mem - 1] / pick(square[mem - 1], mem - 1)
    by_diff = scale * by_diff
    on_steps = jnp.zeros((mem, LANES), F32)
    on_diffs = jnp.zeros((mem, LANES), F32)
    for i in range(mem):
        extra = jnp.sum(on_steps * cross[i], axis=0, keepdims=True)
        beta = inverse[i] * (pick(by_diff, i) + extra)
        on_steps = jnp.where(place == i, alphas[i] - beta, on_steps)
        on_diffs = jnp.where(place == i, -scale * alphas[i], on_diffs)
    return scale, on_diffs, on_steps


def direction_kernel(grams_ref, gradient_ref, steps_hbm, diffs_hbm, out_ref,
                     steps, diffs, load_sems, held, send_sems, recv_sems):
    mem, width = steps.shape
    pairs = load(steps_hbm, diffs_hbm, steps, diffs, load_sems)
    near, far = lax.axis_size("table"), lax.axis_size("dp")
    column, row = lax.axis_index("table"), lax.axis_index("dp")
    peers = [
        {"dp": lax.rem(row + down, far), "table": lax.rem(column + across, near)}
        for down in range(far)
        for across in range(near)
        if down or across
    ]
    barrier = pltpu.get_barrier_semaphore()
    for peer in peers:
        pl.semaphore_signal(barrier, inc=1, device_id=peer, device_id_type=MESH)

    def product(number, carry):
        by_step, by_diff = carry
        for i in range(8):
            at = pl.ds(pl.multiple_of(number * 8 * LANES, LANES) + i * LANES, LANES)
            line = jnp.broadcast_to(gradient_ref[pl.ds(number * 8 + i, 1), :], (mem, LANES))
            by_step = by_step + steps[:, at] * line
            by_diff = by_diff + diffs[:, at] * line
        return by_step, by_diff

    carry = (jnp.zeros((mem, LANES), F32),) * 2
    each = width // len(pairs) // (8 * LANES)
    for part, pair in enumerate(pairs):
        for copy in pair:
            copy.wait()
        carry = lax.fori_loop(part * each, (part + 1) * each, product, carry)
    me = row * near + column
    held[me, 0:1] = grams_ref[...]
    held[me, 1:2] = to_row(carry)
    pl.semaphore_wait(barrier, len(peers))
    total = finish(send(held.at[me], held.at[me], peers, send_sems, recv_sems), held)
    scale, on_diffs, on_steps = coefficients(total[0:1], total[1:2], mem)
    scale, on_diffs, on_steps = -scale, -on_diffs, -on_steps

    def body(number, _):
        rows = []
        for i in range(8):
            at = pl.ds(pl.multiple_of(number * 8 * LANES, LANES) + i * LANES, LANES)
            rows.append(jnp.sum(on_diffs * diffs[:, at] + on_steps * steps[:, at], axis=0, keepdims=True))
        at = pl.ds(pl.multiple_of(number * 8, 8), 8)
        out_ref[at, :] = scale * gradient_ref[at, :] + jnp.concatenate(rows, axis=0)
        return 0

    lax.fori_loop(0, out_ref.shape[0] // 8, body, 0, unroll=2)


def directions(grams, gradient, steps, diffs):
    mem, width = steps.shape
    devices = lax.axis_size("dp") * lax.axis_size("table")
    return pl.pallas_call(
        direction_kernel,
        in_specs=[VMEM] * 2 + [HBM] * 2,
        out_specs=VMEM,
        out_shape=jax.ShapeDtypeStruct(gradient.shape, F32),
        scratch_shapes=[
            pltpu.VMEM((mem, width), F32),
            pltpu.VMEM((mem, width), F32),
            pltpu.SemaphoreType.DMA((2, 4)),
            pltpu.VMEM((devices, 2, LANES), F32),
            pltpu.SemaphoreType.DMA((devices - 1,)),
            pltpu.SemaphoreType.DMA((devices - 1,)),
        ],
        compiler_params=pltpu.CompilerParams(
            vmem_limit_bytes=BUDGET, collective_id=2, has_side_effects=True
        ),
        name="direction",
    )(grams, gradient, steps, diffs)


def local(feature_high, feature_low, labels, weights, history_steps, history_diffs):
    width = weights.shape[0]
    parts = lax.axis_size("dp")
    count = width * parts * lax.axis_size("table")
    bits = width.bit_length() - 1
    slots = feature_high.shape[0]
    subs = parts * feature_high.shape[1] // 1024
    table = weights.reshape(width // LANES, LANES)
    every, partial_gram = share(feature_high, feature_low, labels, history_steps, history_diffs)
    margin, listed, levels = margins(every, table, count, subs, bits, slots)
    total, grams = reduced(margin, partial_gram, history_steps, history_diffs)
    gradient = gradients(total, every, listed, levels, table, subs, bits, 2 * slots)
    return directions(grams, gradient, history_steps, history_diffs).reshape(-1)


def solution(mesh):
    placed = (
        P(None, "dp"),
        P(None, "dp"),
        P("dp"),
        P(("dp", "table")),
        P(None, ("dp", "table")),
        P(None, ("dp", "table")),
    )
    return jax.shard_map(
        local, mesh=mesh, in_specs=placed, out_specs=P(("dp", "table")), check_vma=False
    )
```

```python
import functools

import jax
import jax.numpy as jnp
from jax import lax
from jax.experimental import pallas as pl
from jax.experimental.pallas import tpu as pltpu
from jax.sharding import PartitionSpec as P

HASHES = 4
LANES = 128
BLOCK = 16
GROUP = 4

high_mult = (40503, 96469, 255361, 362443)
low_mult = (2053, 6151, 12289, 98317)
slot_mult = (1543, 3079, 769, 3457)
shifts = (0, 1048573, 2097143, 3145727)
l2_weight = 1.0
BUDGET = 50 << 20
F32, BF16, I32 = jnp.float32, jnp.bfloat16, jnp.int32
MESH = pl.DeviceIdType.MESH
VMEM = pl.BlockSpec(memory_space=pltpu.VMEM)
HBM = pl.BlockSpec(memory_space=pltpu.HBM)
SMEM = pl.BlockSpec(memory_space=pltpu.SMEM)


def iota(shape, axis):
    return lax.broadcasted_iota(I32, shape, axis)


def split(value):
    top = value.astype(BF16)
    return top, (value - top.astype(F32)).astype(BF16)


def hot(index, count):
    shape = (count, index.shape[1])
    return jnp.where(iota(shape, 0) == index, 1.0, 0.0).astype(BF16)


def greet(peers):
    barrier = pltpu.get_barrier_semaphore()
    for peer in peers:
        pl.semaphore_signal(barrier, inc=1, device_id=peer, device_id_type=MESH)
    pl.semaphore_wait(barrier, len(peers))


def others(axis):
    size, me = lax.axis_size(axis), lax.axis_index(axis)
    return [{axis: lax.rem(me + step, size)} for step in range(1, size)]


def send(source, target, peers, send_sems, recv_sems):
    copies = []
    for number, peer in enumerate(peers):
        copy = pltpu.make_async_remote_copy(
            src_ref=source,
            dst_ref=target,
            send_sem=send_sems.at[number],
            recv_sem=recv_sems.at[number],
            device_id=peer,
            device_id_type=MESH,
        )
        copy.start()
        copies.append(copy)
    return copies


def stage(axis, held, value, sems):
    me = lax.axis_index(axis)
    held[me] = value
    return send(held.at[me], held.at[me], others(axis), *sems)


def finish(copies, held):
    for copy in copies:
        copy.wait()
    total = held[0]
    for number in range(1, held.shape[0]):
        total = total + held[number]
    return total


def sum_scratch(shape):
    near, far = lax.axis_size("table"), lax.axis_size("dp")
    return [
        pltpu.VMEM((near, *shape), F32),
        pltpu.VMEM((far, *shape), F32),
        pltpu.SemaphoreType.DMA((near - 1,)),
        pltpu.SemaphoreType.DMA((near - 1,)),
        pltpu.SemaphoreType.DMA((far - 1,)),
        pltpu.SemaphoreType.DMA((far - 1,)),
    ]


def load(steps_hbm, diffs_hbm, steps, diffs, sems, first=0):
    parts, width = sems.shape[1], steps.shape[1]
    pairs = []
    for part in range(parts):
        size = width // parts
        pair = []
        for kind, (source, target) in enumerate(((steps_hbm, steps), (diffs_hbm, diffs))):
            copy = pltpu.make_async_copy(
                source.at[:, pl.ds(first + part * size, size)],
                target.at[:, pl.ds(part * size, size)],
                sems.at[kind, part],
            )
            copy.start()
            pair.append(copy)
        pairs.append(pair)
    return pairs


def gram_part(steps, diffs, pairs, part, carry):
    mem = steps.shape[0]
    each = steps.shape[1] // len(pairs) // LANES
    for copy in pairs[part]:
        copy.wait()

    def body(number, carry):
        at = pl.ds(pl.multiple_of(number * LANES, LANES), LANES)
        step, diff = steps[:, at], diffs[:, at]
        new = []
        for i in range(mem):
            row = jnp.broadcast_to(diffs[i : i + 1, at], diff.shape)
            new.append(carry[2 * i] + step * row)
            new.append(carry[2 * i + 1] + diff * row)
        return tuple(new)

    return lax.fori_loop(part * each, (part + 1) * each, body, carry, unroll=4)


def to_row(columns):
    mem = columns[0].shape[0]
    total = jnp.zeros((mem, LANES), F32)
    spot = iota((mem, LANES), 1) - iota((mem, LANES), 0)
    for number, column in enumerate(columns):
        total = jnp.where(spot == number * mem, jnp.sum(column, axis=1, keepdims=True), total)
    return jnp.sum(total, axis=0, keepdims=True)


def from_row(row, number, mem):
    spot = iota((mem, LANES), 1) - iota((mem, LANES), 0)
    wide = jnp.broadcast_to(row, (mem, LANES))
    column = jnp.sum(jnp.where(spot == number * mem, wide, 0.0), axis=1, keepdims=True)
    return jnp.broadcast_to(column, (mem, LANES))


def gram_row(carry, mem):
    return to_row([carry[2 * i] for i in range(mem)] + [carry[2 * i + 1] for i in range(mem)])


def share_kernel(high_ref, low_ref, labels_ref, steps_hbm, diffs_hbm, every_ref, gram_ref,
                 steps, diffs, send_sems, recv_sems, sems):
    mem = steps.shape[0]
    slots = high_ref.shape[0]
    pairs = load(steps_hbm, diffs_hbm, steps, diffs, sems)
    me = lax.axis_index("dp")
    every_ref[me, :slots] = high_ref[...]
    every_ref[me, slots : 2 * slots] = low_ref[...]
    every_ref[me, 2 * slots : 2 * slots + 1] = labels_ref[...]
    if every_ref.shape[1] > 2 * slots + 1:
        rest = every_ref.shape[1] - 2 * slots - 1
        every_ref[me, 2 * slots + 1 :] = jnp.zeros((rest, labels_ref.shape[1]), I32)
    peers = others("dp")
    greet(peers)
    sent = send(every_ref.at[me], every_ref.at[me], peers, send_sems, recv_sems)
    carry = (jnp.zeros((mem, LANES), F32),) * (2 * mem)
    for part in range(len(pairs)):
        carry = gram_part(steps, diffs, pairs, part, carry)
    gram_ref[...] = gram_row(carry, mem)
    for copy in sent:
        copy.wait()


def share(high, low, labels, steps, diffs):
    mem, width = steps.shape
    rows = -(-(2 * high.shape[0] + 1) // 8) * 8
    dp = lax.axis_size("dp")
    return pl.pallas_call(
        share_kernel,
        in_specs=[VMEM] * 3 + [HBM] * 2,
        out_specs=[VMEM] * 2,
        out_shape=[
            jax.ShapeDtypeStruct((dp, rows, high.shape[1]), I32),
            jax.ShapeDtypeStruct((1, LANES), F32),
        ],
        scratch_shapes=[
            pltpu.VMEM((mem, 3 * width // 4), F32),
            pltpu.VMEM((mem, 3 * width // 4), F32),
            pltpu.SemaphoreType.DMA((dp - 1,)),
            pltpu.SemaphoreType.DMA((dp - 1,)),
            pltpu.SemaphoreType.DMA((2, 3)),
        ],
        compiler_params=pltpu.CompilerParams(
            vmem_limit_bytes=BUDGET, collective_id=0, has_side_effects=True
        ),
        name="share",
    )(high, low, labels.reshape(1, -1), steps, diffs)


def reduce_kernel(margin_ref, gram_ref, steps_hbm, diffs_hbm, out_ref, grams_ref,
                  steps, diffs, load_sems, near, far, *sems):
    mem, size = steps.shape
    pairs = load(steps_hbm, diffs_hbm, steps, diffs, load_sems, steps_hbm.shape[1] - size)
    greet(others("table") + others("dp"))
    carry = (jnp.zeros((mem, LANES), F32),) * (2 * mem)
    copies = stage("table", near, margin_ref[...], sems[:2])
    carry = gram_part(steps, diffs, pairs, 0, carry)
    copies = stage("dp", far, finish(copies, near), sems[2:])
    grams_ref[...] = gram_ref[...] + gram_row(carry, mem)
    out_ref[...] = finish(copies, far)


def reduced(margin, grams, steps, diffs):
    mem, width = steps.shape
    return pl.pallas_call(
        reduce_kernel,
        in_specs=[VMEM] * 2 + [HBM] * 2,
        out_specs=[VMEM] * 2,
        out_shape=[
            jax.ShapeDtypeStruct(margin.shape, F32),
            jax.ShapeDtypeStruct((1, LANES), F32),
        ],
        scratch_shapes=[
            pltpu.VMEM((mem, width // 4), F32),
            pltpu.VMEM((mem, width // 4), F32),
            pltpu.SemaphoreType.DMA((2, 1)),
        ]
        + sum_scratch(margin.shape),
        compiler_params=pltpu.CompilerParams(
            vmem_limit_bytes=BUDGET, collective_id=1, has_side_effects=True
        ),
        name="reduce",
    )(margin, grams, steps, diffs)


def margin_kernel(count, subs, bits, slot_total, every_ref, weights_ref, margin_ref, slots_ref, levels_ref, table, features):
    device = lax.axis_index("dp") * lax.axis_size("table") + lax.axis_index("table")
    width = 1 << bits
    for number in range(2 * slot_total):
        features[number] = every_ref[:, number, :]
    tops, rests = split(weights_ref[...].T)
    table[: LANES] = tops
    table[LANES :] = rests

    def one_pass(number, _):
        base = number * BLOCK

        def body(slot, carry):
            seen, outs = carry[0], list(carry[1:])
            for sub in range(subs):
                group, half = sub // 2, sub % 2
                at = (pl.ds(group * 8, 8), pl.ds(half * LANES, LANES))
                high, low = features[(slot, *at)], features[(slot + slot_total, *at)]
                for k in range(HASHES):
                    index = (high * high_mult[k] + low * low_mult[k] + (slot * slot_mult[k] + shifts[k])) & (count - 1)
                    owned = (index >> bits) == device
                    place = jnp.where(owned, seen, -1)
                    code = (index & (width - 1)) | (sub << bits)
                    for level in range(BLOCK):
                        outs[level] = jnp.where(place == level, code, outs[level])
                    seen = seen + owned.astype(I32)
            return (seen, *outs)

        empty = jnp.full((8, LANES), -1, I32)
        final = lax.fori_loop(0, slot_total, body, (jnp.zeros((8, LANES), I32) - base,) + (empty,) * BLOCK)
        for level in range(BLOCK):
            slots_ref[:, base + level, :] = final[1 + level]
        return final[0] + base

    seen = one_pass(0, None)
    most = jnp.max(seen)
    lax.fori_loop(1, (most + BLOCK - 1) // BLOCK, lambda n, c: (one_pass(n, None), c)[1], 0)
    for row in range(8):
        levels_ref[row] = (jnp.max(seen[row : row + 1]) + GROUP - 1) // GROUP

    def rows(row, _):
        def body(number, total):
            codes = slots_ref[row, pl.ds(number * GROUP, GROUP), :]
            code = jnp.concatenate([codes[i : i + 1] for i in range(GROUP)], axis=1)
            local = code & (width - 1)
            found = jnp.dot(table[...], hot(local >> 7, width // LANES), preferred_element_type=F32)
            found = found[:LANES] + found[LANES:]
            chosen = jnp.where(iota(found.shape, 0) == (local & (LANES - 1)), found, 0.0)
            value = jnp.sum(chosen, axis=0, keepdims=True)
            sub = code >> bits
            for i in range(GROUP):
                at = slice(i * LANES, (i + 1) * LANES)
                total = total + jnp.where(iota((subs, LANES), 0) == sub[:, at], value[:, at], 0.0)
            return total

        total = lax.fori_loop(0, levels_ref[row], body, jnp.zeros((subs, LANES), F32))
        for sub in range(subs):
            here = iota((8, LANES), 0) == row
            margin_ref[sub] = jnp.where(here, total[sub : sub + 1], margin_ref[sub])
        return 0

    margin_ref[...] = jnp.zeros_like(margin_ref)
    lax.fori_loop(0, 8, rows, 0)


def margins(every, weights, count, subs, bits, slots):
    levels = -(-subs * HASHES * slots // BLOCK) * BLOCK
    return pl.pallas_call(
        functools.partial(margin_kernel, count, subs, bits, slots),
        in_specs=[VMEM] * 2,
        out_specs=[VMEM, VMEM, SMEM],
        out_shape=[
            jax.ShapeDtypeStruct((subs, 8, LANES), F32),
            jax.ShapeDtypeStruct((8, levels, LANES), I32),
            jax.ShapeDtypeStruct((8,), I32),
        ],
        scratch_shapes=[
            pltpu.VMEM((2 * LANES, (1 << bits) // LANES), BF16),
            pltpu.VMEM((2 * slots, every.shape[0], every.shape[2]), I32),
        ],
        compiler_params=pltpu.CompilerParams(vmem_limit_bytes=BUDGET),
        name="margins",
    )(every, weights)


def gradient_kernel(subs, bits, label_row, total_ref, every_ref, slots_ref, levels_ref, weights_ref,
                    gradient_ref, residual, both):
    width = 1 << bits
    for sub in range(subs):
        label = every_ref[sub // 2 * 8 : sub // 2 * 8 + 8, label_row, sub % 2 * LANES : sub % 2 * LANES + LANES]
        residual[:, sub, :] = 1.0 / (1.0 + jnp.exp(-total_ref[sub])) - label.astype(F32)
    both[...] = jnp.zeros_like(both)

    def rows(row, _):
        value = residual[row]

        def body(number, _):
            codes = slots_ref[row, pl.ds(number * GROUP, GROUP), :]
            code = jnp.concatenate([codes[i : i + 1] for i in range(GROUP)], axis=1)
            local = code & (width - 1)
            sub = code >> bits
            wide = jnp.concatenate([value] * GROUP, axis=1)
            mine = jnp.sum(jnp.where(iota(wide.shape, 0) == sub, wide, 0.0), axis=0, keepdims=True)
            column = iota((LANES, GROUP * LANES), 0) == (local & (LANES - 1))
            top, rest = split(jnp.where(column, mine, 0.0))
            terms = jnp.concatenate([top, rest], axis=0)
            both[...] += lax.dot_general(
                hot(local >> 7, width // LANES), terms, (((1,), (1,)), ((), ())), preferred_element_type=F32
            )
            return 0

        lax.fori_loop(0, levels_ref[row], body, 0)
        return 0

    lax.fori_loop(0, 8, rows, 0)
    gradient_ref[...] = both[:, :LANES] + both[:, LANES:] + l2_weight * weights_ref[...]


def gradients(total, every, slots, levels, weights, subs, bits, label_row):
    return pl.pallas_call(
        functools.partial(gradient_kernel, subs, bits, label_row),
        in_specs=[VMEM, VMEM, VMEM, SMEM, VMEM],
        out_specs=VMEM,
        out_shape=jax.ShapeDtypeStruct(weights.shape, F32),
        scratch_shapes=[
            pltpu.VMEM((8, subs, LANES), F32),
            pltpu.VMEM((weights.shape[0], 2 * LANES), F32),
        ],
        compiler_params=pltpu.CompilerParams(vmem_limit_bytes=BUDGET),
        name="gradient",
    )(total, every, slots, levels, weights)


def coefficients(grams, products, mem):
    place = iota((mem, LANES), 0)

    def pick(array, number):
        return jnp.broadcast_to(array[number : number + 1], (mem, LANES))

    cross = [from_row(grams, i, mem) for i in range(mem)]
    square = [from_row(grams, mem + i, mem) for i in range(mem)]
    pairs = [pick(cross[i], i) for i in range(mem)]
    inverse = [1.0 / pair for pair in pairs]
    by_step, by_diff = from_row(products, 0, mem), from_row(products, 1, mem)
    alphas = [None] * mem
    for i in reversed(range(mem)):
        alphas[i] = inverse[i] * pick(by_step, i)
        by_step = by_step - alphas[i] * cross[i]
        by_diff = by_diff - alphas[i] * square[i]
    scale = pairs[mem - 1] / pick(square[mem - 1], mem - 1)
    by_diff = scale * by_diff
    on_steps = jnp.zeros((mem, LANES), F32)
    on_diffs = jnp.zeros((mem, LANES), F32)
    for i in range(mem):
        extra = jnp.sum(on_steps * cross[i], axis=0, keepdims=True)
        beta = inverse[i] * (pick(by_diff, i) + extra)
        on_steps = jnp.where(place == i, alphas[i] - beta, on_steps)
        on_diffs = jnp.where(place == i, -scale * alphas[i], on_diffs)
    return scale, on_diffs, on_steps


def row_sums(tiles):
    place = iota((8, LANES), 0)
    gap = 1
    while len(tiles) > 1:
        low = (place & gap) == 0
        tiles = [
            jnp.where(low, a, b) + pltpu.roll(jnp.where(low, b, a), 8 - gap, 0)
            for a, b in zip(tiles[::2], tiles[1::2])
        ]
        gap *= 2
    return tiles[0]


def direction_kernel(grams_ref, gradient_ref, steps_hbm, diffs_hbm, out_ref,
                     steps, diffs, load_sems, held, send_sems, recv_sems):
    mem, width = steps.shape
    pairs = load(steps_hbm, diffs_hbm, steps, diffs, load_sems)
    near, far = lax.axis_size("table"), lax.axis_size("dp")
    column, row = lax.axis_index("table"), lax.axis_index("dp")
    peers = [
        {"dp": lax.rem(row + down, far), "table": lax.rem(column + across, near)}
        for down in range(far)
        for across in range(near)
        if down or across
    ]
    barrier = pltpu.get_barrier_semaphore()
    for peer in peers:
        pl.semaphore_signal(barrier, inc=1, device_id=peer, device_id_type=MESH)

    def product(number, carry):
        by_step, by_diff = carry
        for i in range(8):
            at = pl.ds(pl.multiple_of(number * 8 * LANES, LANES) + i * LANES, LANES)
            line = jnp.broadcast_to(gradient_ref[pl.ds(number * 8 + i, 1), :], (mem, LANES))
            by_step = by_step + steps[:, at] * line
            by_diff = by_diff + diffs[:, at] * line
        return by_step, by_diff

    carry = (jnp.zeros((mem, LANES), F32),) * 2
    each = width // len(pairs) // (8 * LANES)
    for part, pair in enumerate(pairs):
        for copy in pair:
            copy.wait()
        carry = lax.fori_loop(part * each, (part + 1) * each, product, carry)
    me = row * near + column
    held[me, 0:1] = grams_ref[...]
    held[me, 1:2] = to_row(carry)
    pl.semaphore_wait(barrier, len(peers))
    total = finish(send(held.at[me], held.at[me], peers, send_sems, recv_sems), held)
    scale, on_diffs, on_steps = coefficients(total[0:1], total[1:2], mem)
    scale, on_diffs, on_steps = -scale, -on_diffs, -on_steps

    def body(number, _):
        rows = []
        for i in range(8):
            at = pl.ds(pl.multiple_of(number * 8 * LANES, LANES) + i * LANES, LANES)
            rows.append(on_diffs * diffs[:, at] + on_steps * steps[:, at])
        at = pl.ds(pl.multiple_of(number * 8, 8), 8)
        out_ref[at, :] = scale * gradient_ref[at, :] + row_sums(rows)
        return 0

    lax.fori_loop(0, out_ref.shape[0] // 8, body, 0, unroll=2)


def directions(grams, gradient, steps, diffs):
    mem, width = steps.shape
    devices = lax.axis_size("dp") * lax.axis_size("table")
    return pl.pallas_call(
        direction_kernel,
        in_specs=[VMEM] * 2 + [HBM] * 2,
        out_specs=VMEM,
        out_shape=jax.ShapeDtypeStruct(gradient.shape, F32),
        scratch_shapes=[
            pltpu.VMEM((mem, width), F32),
            pltpu.VMEM((mem, width), F32),
            pltpu.SemaphoreType.DMA((2, 4)),
            pltpu.VMEM((devices, 2, LANES), F32),
            pltpu.SemaphoreType.DMA((devices - 1,)),
            pltpu.SemaphoreType.DMA((devices - 1,)),
        ],
        compiler_params=pltpu.CompilerParams(
            vmem_limit_bytes=BUDGET, collective_id=2, has_side_effects=True
        ),
        name="direction",
    )(grams, gradient, steps, diffs)


def local(feature_high, feature_low, labels, weights, history_steps, history_diffs):
    width = weights.shape[0]
    parts = lax.axis_size("dp")
    count = width * parts * lax.axis_size("table")
    bits = width.bit_length() - 1
    slots = feature_high.shape[0]
    subs = parts * feature_high.shape[1] // 1024
    table = weights.reshape(width // LANES, LANES)
    every, partial_gram = share(feature_high, feature_low, labels, history_steps, history_diffs)
    margin, listed, levels = margins(every, table, count, subs, bits, slots)
    total, grams = reduced(margin, partial_gram, history_steps, history_diffs)
    gradient = gradients(total, every, listed, levels, table, subs, bits, 2 * slots)
    return directions(grams, gradient, history_steps, history_diffs).reshape(-1)


def solution(mesh):
    placed = (
        P(None, "dp"),
        P(None, "dp"),
        P("dp"),
        P(("dp", "table")),
        P(None, ("dp", "table")),
        P(None, ("dp", "table")),
    )
    return jax.shard_map(
        local, mesh=mesh, in_specs=placed, out_specs=P(("dp", "table")), check_vma=False
    )
```

```python
import functools

import jax
import jax.numpy as jnp
from jax import lax
from jax.experimental import pallas as pl
from jax.experimental.pallas import tpu as pltpu
from jax.sharding import PartitionSpec as P

HASHES = 4
LANES = 128
BLOCK = 16
GROUP = 4

high_mult = (40503, 96469, 255361, 362443)
low_mult = (2053, 6151, 12289, 98317)
slot_mult = (1543, 3079, 769, 3457)
shifts = (0, 1048573, 2097143, 3145727)
l2_weight = 1.0
BUDGET = 50 << 20
F32, BF16, I32 = jnp.float32, jnp.bfloat16, jnp.int32
MESH = pl.DeviceIdType.MESH
VMEM = pl.BlockSpec(memory_space=pltpu.VMEM)
HBM = pl.BlockSpec(memory_space=pltpu.HBM)
SMEM = pl.BlockSpec(memory_space=pltpu.SMEM)


def iota(shape, axis):
    return lax.broadcasted_iota(I32, shape, axis)


def split(value):
    top = value.astype(BF16)
    return top, (value - top.astype(F32)).astype(BF16)


def hot(index, count):
    shape = (count, index.shape[1])
    return jnp.where(iota(shape, 0) == index, 1.0, 0.0).astype(BF16)


def greet(peers):
    barrier = pltpu.get_barrier_semaphore()
    for peer in peers:
        pl.semaphore_signal(barrier, inc=1, device_id=peer, device_id_type=MESH)
    pl.semaphore_wait(barrier, len(peers))


def others(axis):
    size, me = lax.axis_size(axis), lax.axis_index(axis)
    return [{axis: lax.rem(me + step, size)} for step in range(1, size)]


def send(source, target, peers, send_sems, recv_sems):
    copies = []
    for number, peer in enumerate(peers):
        copy = pltpu.make_async_remote_copy(
            src_ref=source,
            dst_ref=target,
            send_sem=send_sems.at[number],
            recv_sem=recv_sems.at[number],
            device_id=peer,
            device_id_type=MESH,
        )
        copy.start()
        copies.append(copy)
    return copies


def stage(axis, held, value, sems):
    me = lax.axis_index(axis)
    held[me] = value
    return send(held.at[me], held.at[me], others(axis), *sems)


def finish(copies, held):
    for copy in copies:
        copy.wait()
    total = held[0]
    for number in range(1, held.shape[0]):
        total = total + held[number]
    return total


def sum_scratch(shape):
    near, far = lax.axis_size("table"), lax.axis_size("dp")
    return [
        pltpu.VMEM((near, *shape), F32),
        pltpu.VMEM((far, *shape), F32),
        pltpu.SemaphoreType.DMA((near - 1,)),
        pltpu.SemaphoreType.DMA((near - 1,)),
        pltpu.SemaphoreType.DMA((far - 1,)),
        pltpu.SemaphoreType.DMA((far - 1,)),
    ]


def load(steps_hbm, diffs_hbm, steps, diffs, sems, first=0):
    parts, width = sems.shape[1], steps.shape[1]
    pairs = []
    for part in range(parts):
        size = width // parts
        pair = []
        for kind, (source, target) in enumerate(((steps_hbm, steps), (diffs_hbm, diffs))):
            copy = pltpu.make_async_copy(
                source.at[:, pl.ds(first + part * size, size)],
                target.at[:, pl.ds(part * size, size)],
                sems.at[kind, part],
            )
            copy.start()
            pair.append(copy)
        pairs.append(pair)
    return pairs


def gram_part(steps, diffs, pairs, part, carry):
    mem = steps.shape[0]
    each = steps.shape[1] // len(pairs) // LANES
    for copy in pairs[part]:
        copy.wait()

    def body(number, carry):
        at = pl.ds(pl.multiple_of(number * LANES, LANES), LANES)
        step, diff = steps[:, at], diffs[:, at]
        new = []
        for i in range(mem):
            row = jnp.broadcast_to(diffs[i : i + 1, at], diff.shape)
            new.append(carry[2 * i] + step * row)
            new.append(carry[2 * i + 1] + diff * row)
        return tuple(new)

    return lax.fori_loop(part * each, (part + 1) * each, body, carry, unroll=4)


def to_row(columns):
    mem = columns[0].shape[0]
    total = jnp.zeros((mem, LANES), F32)
    spot = iota((mem, LANES), 1) - iota((mem, LANES), 0)
    for number, column in enumerate(columns):
        total = jnp.where(spot == number * mem, jnp.sum(column, axis=1, keepdims=True), total)
    return jnp.sum(total, axis=0, keepdims=True)


def from_row(row, number, mem):
    spot = iota((mem, LANES), 1) - iota((mem, LANES), 0)
    wide = jnp.broadcast_to(row, (mem, LANES))
    column = jnp.sum(jnp.where(spot == number * mem, wide, 0.0), axis=1, keepdims=True)
    return jnp.broadcast_to(column, (mem, LANES))


def gram_row(carry, mem):
    return to_row([carry[2 * i] for i in range(mem)] + [carry[2 * i + 1] for i in range(mem)])


def share_kernel(mine_ref, steps_hbm, diffs_hbm, every_ref, gram_ref,
                 steps, diffs, send_sems, recv_sems, sems):
    mem = steps.shape[0]
    pairs = load(steps_hbm, diffs_hbm, steps, diffs, sems)
    me = lax.axis_index("dp")
    every_ref[me] = mine_ref[...]
    peers = others("dp")
    greet(peers)
    sent = send(mine_ref, every_ref.at[me], peers, send_sems, recv_sems)
    carry = (jnp.zeros((mem, LANES), F32),) * (2 * mem)
    for part in range(len(pairs)):
        carry = gram_part(steps, diffs, pairs, part, carry)
    gram_ref[...] = gram_row(carry, mem)
    for copy in sent:
        copy.wait()


def share(mine, steps, diffs):
    mem, width = steps.shape
    dp = lax.axis_size("dp")
    return pl.pallas_call(
        share_kernel,
        in_specs=[VMEM] + [HBM] * 2,
        out_specs=[VMEM] * 2,
        out_shape=[
            jax.ShapeDtypeStruct((dp, *mine.shape), I32),
            jax.ShapeDtypeStruct((1, LANES), F32),
        ],
        scratch_shapes=[
            pltpu.VMEM((mem, 3 * width // 4), F32),
            pltpu.VMEM((mem, 3 * width // 4), F32),
            pltpu.SemaphoreType.DMA((dp - 1,)),
            pltpu.SemaphoreType.DMA((dp - 1,)),
            pltpu.SemaphoreType.DMA((2, 3)),
        ],
        compiler_params=pltpu.CompilerParams(
            vmem_limit_bytes=BUDGET, collective_id=0, has_side_effects=True
        ),
        name="share",
    )(mine, steps, diffs)


def reduce_kernel(margin_ref, gram_ref, steps_hbm, diffs_hbm, out_ref, grams_ref,
                  steps, diffs, load_sems, near, far, *sems):
    mem, size = steps.shape
    pairs = load(steps_hbm, diffs_hbm, steps, diffs, load_sems, steps_hbm.shape[1] - size)
    greet(others("table") + others("dp"))
    carry = (jnp.zeros((mem, LANES), F32),) * (2 * mem)
    copies = stage("table", near, margin_ref[...], sems[:2])
    copies = stage("dp", far, finish(copies, near), sems[2:])
    carry = gram_part(steps, diffs, pairs, 0, carry)
    grams_ref[...] = gram_ref[...] + gram_row(carry, mem)
    out_ref[...] = finish(copies, far)


def reduced(margin, grams, steps, diffs):
    mem, width = steps.shape
    return pl.pallas_call(
        reduce_kernel,
        in_specs=[VMEM] * 2 + [HBM] * 2,
        out_specs=[VMEM] * 2,
        out_shape=[
            jax.ShapeDtypeStruct(margin.shape, F32),
            jax.ShapeDtypeStruct((1, LANES), F32),
        ],
        scratch_shapes=[
            pltpu.VMEM((mem, width // 4), F32),
            pltpu.VMEM((mem, width // 4), F32),
            pltpu.SemaphoreType.DMA((2, 1)),
        ]
        + sum_scratch(margin.shape),
        compiler_params=pltpu.CompilerParams(
            vmem_limit_bytes=BUDGET, collective_id=1, has_side_effects=True
        ),
        name="reduce",
    )(margin, grams, steps, diffs)


def margin_kernel(count, subs, bits, slot_total, every_ref, weights_ref, margin_ref, slots_ref, levels_ref, table, features):
    device = lax.axis_index("dp") * lax.axis_size("table") + lax.axis_index("table")
    width = 1 << bits
    for number in range(2 * slot_total):
        features[number] = every_ref[:, number, :]
    tops, rests = split(weights_ref[...].T)
    table[: LANES] = tops
    table[LANES :] = rests

    def one_pass(number, _):
        base = number * BLOCK

        def body(slot, carry):
            seen, outs = carry[0], list(carry[1:])
            for sub in range(subs):
                group, half = sub // 2, sub % 2
                at = (pl.ds(group * 8, 8), pl.ds(half * LANES, LANES))
                high, low = features[(slot, *at)], features[(slot + slot_total, *at)]
                for k in range(HASHES):
                    index = (high * high_mult[k] + low * low_mult[k] + (slot * slot_mult[k] + shifts[k])) & (count - 1)
                    owned = (index >> bits) == device
                    place = jnp.where(owned, seen, -1)
                    code = (index & (width - 1)) | (sub << bits)
                    for level in range(BLOCK):
                        outs[level] = jnp.where(place == level, code, outs[level])
                    seen = seen + owned.astype(I32)
            return (seen, *outs)

        empty = jnp.full((8, LANES), -1, I32)
        final = lax.fori_loop(0, slot_total, body, (jnp.zeros((8, LANES), I32) - base,) + (empty,) * BLOCK)
        for level in range(BLOCK):
            slots_ref[:, base + level, :] = final[1 + level]
        return final[0] + base

    seen = one_pass(0, None)
    most = jnp.max(seen)
    lax.fori_loop(1, (most + BLOCK - 1) // BLOCK, lambda n, c: (one_pass(n, None), c)[1], 0)
    for row in range(8):
        levels_ref[row] = (jnp.max(seen[row : row + 1]) + GROUP - 1) // GROUP

    def rows(row, _):
        def body(number, total):
            codes = slots_ref[row, pl.ds(number * GROUP, GROUP), :]
            code = jnp.concatenate([codes[i : i + 1] for i in range(GROUP)], axis=1)
            local = code & (width - 1)
            found = jnp.dot(table[...], hot(local >> 7, width // LANES), preferred_element_type=F32)
            found = found[:LANES] + found[LANES:]
            chosen = jnp.where(iota(found.shape, 0) == (local & (LANES - 1)), found, 0.0)
            value = jnp.sum(chosen, axis=0, keepdims=True)
            sub = code >> bits
            for i in range(GROUP):
                at = slice(i * LANES, (i + 1) * LANES)
                total = total + jnp.where(iota((subs, LANES), 0) == sub[:, at], value[:, at], 0.0)
            return total

        total = lax.fori_loop(0, levels_ref[row], body, jnp.zeros((subs, LANES), F32))
        for sub in range(subs):
            here = iota((8, LANES), 0) == row
            margin_ref[sub] = jnp.where(here, total[sub : sub + 1], margin_ref[sub])
        return 0

    margin_ref[...] = jnp.zeros_like(margin_ref)
    lax.fori_loop(0, 8, rows, 0)


def margins(every, weights, count, subs, bits, slots):
    levels = -(-subs * HASHES * slots // BLOCK) * BLOCK
    return pl.pallas_call(
        functools.partial(margin_kernel, count, subs, bits, slots),
        in_specs=[VMEM] * 2,
        out_specs=[VMEM, VMEM, SMEM],
        out_shape=[
            jax.ShapeDtypeStruct((subs, 8, LANES), F32),
            jax.ShapeDtypeStruct((8, levels, LANES), I32),
            jax.ShapeDtypeStruct((8,), I32),
        ],
        scratch_shapes=[
            pltpu.VMEM((2 * LANES, (1 << bits) // LANES), BF16),
            pltpu.VMEM((2 * slots, every.shape[0], every.shape[2]), I32),
        ],
        compiler_params=pltpu.CompilerParams(vmem_limit_bytes=BUDGET),
        name="margins",
    )(every, weights)


def gradient_kernel(subs, bits, label_row, total_ref, every_ref, slots_ref, levels_ref, weights_ref,
                    gradient_ref, residual, both):
    width = 1 << bits
    for sub in range(subs):
        label = every_ref[sub // 2 * 8 : sub // 2 * 8 + 8, label_row, sub % 2 * LANES : sub % 2 * LANES + LANES]
        residual[:, sub, :] = 1.0 / (1.0 + jnp.exp(-total_ref[sub])) - label.astype(F32)
    both[...] = jnp.zeros_like(both)

    def rows(row, _):
        value = residual[row]

        def body(number, _):
            codes = slots_ref[row, pl.ds(number * GROUP, GROUP), :]
            code = jnp.concatenate([codes[i : i + 1] for i in range(GROUP)], axis=1)
            local = code & (width - 1)
            sub = code >> bits
            wide = jnp.concatenate([value] * GROUP, axis=1)
            mine = jnp.sum(jnp.where(iota(wide.shape, 0) == sub, wide, 0.0), axis=0, keepdims=True)
            column = iota((LANES, GROUP * LANES), 0) == (local & (LANES - 1))
            top, rest = split(jnp.where(column, mine, 0.0))
            terms = jnp.concatenate([top, rest], axis=0)
            both[...] += lax.dot_general(
                hot(local >> 7, width // LANES), terms, (((1,), (1,)), ((), ())), preferred_element_type=F32
            )
            return 0

        lax.fori_loop(0, levels_ref[row], body, 0)
        return 0

    lax.fori_loop(0, 8, rows, 0)
    gradient_ref[...] = both[:, :LANES] + both[:, LANES:] + l2_weight * weights_ref[...]


def gradients(total, every, slots, levels, weights, subs, bits, label_row):
    return pl.pallas_call(
        functools.partial(gradient_kernel, subs, bits, label_row),
        in_specs=[VMEM, VMEM, VMEM, SMEM, VMEM],
        out_specs=VMEM,
        out_shape=jax.ShapeDtypeStruct(weights.shape, F32),
        scratch_shapes=[
            pltpu.VMEM((8, subs, LANES), F32),
            pltpu.VMEM((weights.shape[0], 2 * LANES), F32),
        ],
        compiler_params=pltpu.CompilerParams(vmem_limit_bytes=BUDGET),
        name="gradient",
    )(total, every, slots, levels, weights)


def coefficients(grams, products, mem):
    place = iota((mem, LANES), 0)

    def pick(array, number):
        return jnp.broadcast_to(array[number : number + 1], (mem, LANES))

    cross = [from_row(grams, i, mem) for i in range(mem)]
    square = [from_row(grams, mem + i, mem) for i in range(mem)]
    pairs = [pick(cross[i], i) for i in range(mem)]
    inverse = [1.0 / pair for pair in pairs]
    by_step, by_diff = from_row(products, 0, mem), from_row(products, 1, mem)
    alphas = [None] * mem
    for i in reversed(range(mem)):
        alphas[i] = inverse[i] * pick(by_step, i)
        by_step = by_step - alphas[i] * cross[i]
        by_diff = by_diff - alphas[i] * square[i]
    scale = pairs[mem - 1] / pick(square[mem - 1], mem - 1)
    by_diff = scale * by_diff
    on_steps = jnp.zeros((mem, LANES), F32)
    on_diffs = jnp.zeros((mem, LANES), F32)
    for i in range(mem):
        extra = jnp.sum(on_steps * cross[i], axis=0, keepdims=True)
        beta = inverse[i] * (pick(by_diff, i) + extra)
        on_steps = jnp.where(place == i, alphas[i] - beta, on_steps)
        on_diffs = jnp.where(place == i, -scale * alphas[i], on_diffs)
    return scale, on_diffs, on_steps


def row_sums(tiles):
    place = iota((8, LANES), 0)
    gap = 1
    while len(tiles) > 1:
        low = (place & gap) == 0
        tiles = [
            jnp.where(low, a, b) + pltpu.roll(jnp.where(low, b, a), 8 - gap, 0)
            for a, b in zip(tiles[::2], tiles[1::2])
        ]
        gap *= 2
    return tiles[0]


def direction_kernel(grams_ref, gradient_ref, steps_hbm, diffs_hbm, out_ref,
                     steps, diffs, load_sems, held, send_sems, recv_sems):
    mem, width = steps.shape
    pairs = load(steps_hbm, diffs_hbm, steps, diffs, load_sems)
    near, far = lax.axis_size("table"), lax.axis_size("dp")
    column, row = lax.axis_index("table"), lax.axis_index("dp")
    peers = [
        {"dp": lax.rem(row + down, far), "table": lax.rem(column + across, near)}
        for down in range(far)
        for across in range(near)
        if down or across
    ]
    barrier = pltpu.get_barrier_semaphore()
    for peer in peers:
        pl.semaphore_signal(barrier, inc=1, device_id=peer, device_id_type=MESH)

    def product(number, carry):
        by_step, by_diff = carry
        for i in range(8):
            at = pl.ds(pl.multiple_of(number * 8 * LANES, LANES) + i * LANES, LANES)
            line = jnp.broadcast_to(gradient_ref[pl.ds(number * 8 + i, 1), :], (mem, LANES))
            by_step = by_step + steps[:, at] * line
            by_diff = by_diff + diffs[:, at] * line
        return by_step, by_diff

    carry = (jnp.zeros((mem, LANES), F32),) * 2
    each = width // len(pairs) // (8 * LANES)
    for part, pair in enumerate(pairs):
        for copy in pair:
            copy.wait()
        carry = lax.fori_loop(part * each, (part + 1) * each, product, carry)
    me = row * near + column
    held[me, 0:1] = grams_ref[...]
    held[me, 1:2] = to_row(carry)
    pl.semaphore_wait(barrier, len(peers))
    total = finish(send(held.at[me], held.at[me], peers, send_sems, recv_sems), held)
    scale, on_diffs, on_steps = coefficients(total[0:1], total[1:2], mem)
    scale, on_diffs, on_steps = -scale, -on_diffs, -on_steps

    def body(number, _):
        rows = []
        for i in range(8):
            at = pl.ds(pl.multiple_of(number * 8 * LANES, LANES) + i * LANES, LANES)
            rows.append(on_diffs * diffs[:, at] + on_steps * steps[:, at])
        at = pl.ds(pl.multiple_of(number * 8, 8), 8)
        out_ref[at, :] = scale * gradient_ref[at, :] + row_sums(rows)
        return 0

    lax.fori_loop(0, out_ref.shape[0] // 8, body, 0, unroll=2)


def directions(grams, gradient, steps, diffs):
    mem, width = steps.shape
    devices = lax.axis_size("dp") * lax.axis_size("table")
    return pl.pallas_call(
        direction_kernel,
        in_specs=[VMEM] * 2 + [HBM] * 2,
        out_specs=VMEM,
        out_shape=jax.ShapeDtypeStruct(gradient.shape, F32),
        scratch_shapes=[
            pltpu.VMEM((mem, width), F32),
            pltpu.VMEM((mem, width), F32),
            pltpu.SemaphoreType.DMA((2, 4)),
            pltpu.VMEM((devices, 2, LANES), F32),
            pltpu.SemaphoreType.DMA((devices - 1,)),
            pltpu.SemaphoreType.DMA((devices - 1,)),
        ],
        compiler_params=pltpu.CompilerParams(
            vmem_limit_bytes=BUDGET, collective_id=2, has_side_effects=True
        ),
        name="direction",
    )(grams, gradient, steps, diffs)


def local(feature_high, feature_low, labels, weights, history_steps, history_diffs):
    width = weights.shape[0]
    parts = lax.axis_size("dp")
    count = width * parts * lax.axis_size("table")
    bits = width.bit_length() - 1
    slots = feature_high.shape[0]
    subs = parts * feature_high.shape[1] // 1024
    table = weights.reshape(width // LANES, LANES)
    mine = jnp.concatenate([feature_high, feature_low, labels[None, :]], axis=0)
    every, partial_gram = share(mine, history_steps, history_diffs)
    margin, listed, levels = margins(every, table, count, subs, bits, slots)
    total, grams = reduced(margin, partial_gram, history_steps, history_diffs)
    gradient = gradients(total, every, listed, levels, table, subs, bits, 2 * slots)
    return directions(grams, gradient, history_steps, history_diffs).reshape(-1)


def solution(mesh):
    placed = (
        P(None, "dp"),
        P(None, "dp"),
        P("dp"),
        P(("dp", "table")),
        P(None, ("dp", "table")),
        P(None, ("dp", "table")),
    )
    return jax.shard_map(
        local, mesh=mesh, in_specs=placed, out_specs=P(("dp", "table")), check_vma=False
    )
```
